32 devices in a mesh: users: 8 (over z, y), items: 4 (over x, core).
Axes of the slice: x: 2, y: 2, z: 4, core: 2. Of those that a mesh axis runs over, the one named last changes fastest.
Arguments:
- tile_rows: int32 [8, 4, 512], P('users', 'items'), may hold values from 0 to 63, as said below
- tile_cols: int32 [8, 4, 512], P('users', 'items'), may hold values from 0 to 63, as said below
- tile_count: int32 [8, 4], P('users', 'items'), may hold values from 64 to 512, as said below
- tile_vals: bfloat16 [8, 4, 512, 128, 128], P('users', 'items'), may hold values from -6 to 6
- user_degree: int32 [65536], P(('users', 'items')), may hold values from 16 to 575
- item_degree: int32 [32768], P(('items', 'users')), may hold values from 16 to 575
- start_items: bfloat16 [64, 32768], P(None, ('items', 'users')), may hold values from -6 to 6
Outputs:
- user_panel: float32 [64, 65536], P(None, ('users', 'items'))
- item_panel: float32 [64, 32768], P(None, ('items', 'users'))
The draws below stay inside these ranges and needn't reach their ends.
Inputs may be any that keep to these rules, and one draw needn't show every extreme that they name: Within one user block and item block, the pairs (tile_rows, tile_cols) of all 512 slots are distinct. `tile_cols`: paired with tile_rows slot by slot. Only the first tile_count slots of a block are live; some block is full in every draw.
All inputs are finite; a program needn't handle non-finite values.
Results may differ from the reference program's by a relative error of at most 0.0003.
Values sent between devices are 32-bit elements; how exact they have to be, the bound alone decides.
No kernel may reach another device: no remote copies, remote signals or barrier semaphores. Data moves between devices by JAX's collectives and lax.ppermute only.
A program may use at most 128 MiB of HBM per device.

```python
import jax
import jax.numpy as jnp
from jax import lax

K = 64
TILE = 128
ITERS = 2
UT = 64
IT = 64
TILES_DEV = 512
USER_BLOCKS = 8
ITEM_BLOCKS = 4
USERS = 65536
ITEMS = 32768


def tile_slots(key):
    base = jax.random.fold_in(key, 7)
    keys = jax.random.split(base, USER_BLOCKS * ITEM_BLOCKS)
    chosen = jax.vmap(lambda single: jax.random.permutation(single, UT * IT)[:TILES_DEV])(keys)
    return chosen.reshape(USER_BLOCKS, ITEM_BLOCKS, TILES_DEV).astype(jnp.int32)


def draw_tile_rows(key, part):
    return tile_slots(key) // IT


def draw_tile_cols(key, part):
    return tile_slots(key) % IT


def draw_tile_count(key, part):
    first = jax.random.fold_in(key, 11)
    second = jax.random.fold_in(key, 13)
    powers = jax.random.randint(first, (USER_BLOCKS * ITEM_BLOCKS,), 0, 4)
    counts = jnp.maximum(TILES_DEV // jnp.left_shift(jnp.int32(1), powers.astype(jnp.int32)), 1)
    fullest = jax.random.randint(second, (), 0, USER_BLOCKS * ITEM_BLOCKS)
    counts = jnp.where(jnp.arange(USER_BLOCKS * ITEM_BLOCKS) == fullest, TILES_DEV, counts)
    return counts.reshape(USER_BLOCKS, ITEM_BLOCKS).astype(jnp.int32)


def degree_draw(key, total):
    base = jax.random.randint(key, (total,), 16, 64)
    places = jnp.arange(total, dtype=jnp.int32)
    return (base * (total + 8 * places) // total).astype(jnp.int32)


def draw_user_degree(key, part):
    return degree_draw(jax.random.fold_in(key, 17), USERS)


def draw_item_degree(key, part):
    return degree_draw(jax.random.fold_in(key, 19), ITEMS)


def steps_of(stream_key, shape, shards, low, high):
    factor_of = 1.0
    for axis_at, parts in shards:
        heights = jax.random.uniform(jax.random.fold_in(jax.random.fold_in(stream_key, 6), axis_at), (parts,), jnp.float32, low / len(shards), high / len(shards))
        factor_of = factor_of * jnp.repeat(jnp.exp(heights), shape[axis_at] // parts).reshape((-1,) + (1,) * (len(shape) - 1 - axis_at))
    return factor_of


def centred(key, dims, spread, reach, cuts=(), kind=jnp.bfloat16):
    entries = spread * jax.random.normal(key, dims, jnp.float32)
    if cuts:
        entries = entries * steps_of(key, dims, cuts, -0.22, 0.18)
    return jnp.clip(entries, -reach, reach).astype(kind)


def setup_inputs(seed: int = 0) -> dict:
    key_list = jax.random.split(jax.random.key(seed), 8)
    tile_rows = draw_tile_rows(jax.random.fold_in(key_list[7], 71), 0)
    tile_cols = draw_tile_cols(jax.random.fold_in(key_list[7], 71), 0)
    tile_count = draw_tile_count(jax.random.fold_in(key_list[7], 71), 0)
    tile_vals = centred(key_list[3], (USER_BLOCKS, ITEM_BLOCKS, TILES_DEV, TILE, TILE), 1.0, 6.0, ((0, 8), (1, 4)))
    user_degree = draw_user_degree(jax.random.fold_in(key_list[7], 71), 0)
    item_degree = draw_item_degree(jax.random.fold_in(key_list[7], 71), 0)
    start_items = centred(key_list[6], (K, ITEMS), 1.0, 6.0, ((1, 32),))
    return {"tile_rows": tile_rows, "tile_cols": tile_cols, "tile_count": tile_count, "tile_vals": tile_vals, "user_degree": user_degree, "item_degree": item_degree, "start_items": start_items}


def orthonormalize(raw, total):
    gram = jnp.einsum('kr,jr->kj', raw.astype(jnp.float32), raw.astype(jnp.float32), precision=lax.Precision.HIGHEST, preferred_element_type=jnp.float32) / total
    lower = jnp.linalg.cholesky(gram)
    return lax.linalg.triangular_solve(lower, raw, left_side=True, lower=True)

def user_side(sent_items, tile_rows, tile_cols, tile_count, tile_vals):
    blocks = sent_items.reshape(K, ITEM_BLOCKS, IT, TILE)

    def one_user_block(user_block):

        def add_item(total, item_block):
            values = tile_vals[user_block, item_block].astype(jnp.float32)
            rows = tile_rows[user_block, item_block]
            cols = tile_cols[user_block, item_block]
            live = (jnp.arange(TILES_DEV) < tile_count[user_block, item_block]).astype(jnp.float32)
            picked = jnp.take(blocks[:, item_block], cols, axis=1).astype(jnp.float32)
            product = jnp.einsum('ktc,trc->ktr', picked, values, precision=lax.Precision.HIGHEST)
            product = product * live[None, :, None]
            return (total.at[:, rows, :].add(product), None)
        total, _ = lax.scan(add_item, jnp.zeros((K, UT, TILE), jnp.float32), jnp.arange(ITEM_BLOCKS))
        return total
    result = lax.map(one_user_block, jnp.arange(USER_BLOCKS))
    return result.transpose(1, 0, 2, 3).reshape(K, USERS)

def item_side(sent_users, tile_rows, tile_cols, tile_count, tile_vals):
    blocks = sent_users.reshape(K, USER_BLOCKS, UT, TILE)

    def one_item_block(item_block):

        def add_user(total, user_block):
            values = tile_vals[user_block, item_block].astype(jnp.float32)
            rows = tile_rows[user_block, item_block]
            cols = tile_cols[user_block, item_block]
            live = (jnp.arange(TILES_DEV) < tile_count[user_block, item_block]).astype(jnp.float32)
            picked = jnp.take(blocks[:, user_block], rows, axis=1).astype(jnp.float32)
            product = jnp.einsum('ktr,trc->ktc', picked, values, precision=lax.Precision.HIGHEST)
            product = product * live[None, :, None]
            return (total.at[:, cols, :].add(product), None)
        total, _ = lax.scan(add_user, jnp.zeros((K, IT, TILE), jnp.float32), jnp.arange(USER_BLOCKS))
        return total
    result = lax.map(one_item_block, jnp.arange(ITEM_BLOCKS))
    return result.transpose(1, 0, 2, 3).reshape(K, ITEMS)

def reference(tile_rows, tile_cols, tile_count, tile_vals, user_degree, item_degree, start_items):
    user_scale = lax.rsqrt(user_degree.astype(jnp.float32))
    item_scale = lax.rsqrt(item_degree.astype(jnp.float32))
    panel = start_items.astype(jnp.float32)
    user_panel = jnp.zeros((K, USERS), jnp.float32)
    for step in range(ITERS):
        sent_items = item_scale[None, :] * panel
        user_raw = user_scale[None, :] * user_side(sent_items, tile_rows, tile_cols, tile_count, tile_vals)
        user_panel = orthonormalize(user_raw, USERS)
        sent_users = user_scale[None, :] * user_panel
        item_raw = item_scale[None, :] * item_side(sent_users, tile_rows, tile_cols, tile_count, tile_vals)
        panel = orthonormalize(item_raw, ITEMS)
    return (user_panel, panel)
```

```python
import functools

import jax
import jax.numpy as jnp
from jax import lax
from jax.experimental import pallas as pl
from jax.experimental.pallas import tpu as pltpu
from jax.sharding import PartitionSpec as P

K = 64
TILE = 128
ITERS = 2
UT = 64
IT = 64
BATCH = 64
UNROLL = 32
HIGHEST = lax.Precision.HIGHEST


def gather_order(size):
    bits = []
    bit = size >> 1
    while bit:
        bits.append(bit)
        bit >>= 1
    return bits


def exchange(value, axis, bit):
    size = lax.axis_size(axis)
    return lax.ppermute(value, axis, [(at, at ^ bit) for at in range(size)])


def relative_position(shard, axis):
    apart = shard ^ lax.axis_index(axis)
    place = jnp.zeros_like(apart)
    for level, bit in enumerate(gather_order(lax.axis_size(axis))):
        place = place + jnp.where(apart & bit != 0, 1 << level, 0)
    return place


def all_gather_halves(shard, axis):
    held = shard
    order = gather_order(lax.axis_size(axis))
    for bit in order[:-1]:
        held = jnp.concatenate([held, exchange(held, axis, bit)], axis=0)
    return held, exchange(held, axis, order[-1])


def reduce_scatter_halves(kept, sent, axis):
    order = gather_order(lax.axis_size(axis))[::-1]
    received = exchange(sent, axis, order[0])
    for bit in order[1:]:
        half = kept.shape[0] // 2
        sent = kept[half:] + received[half:]
        kept = kept[:half] + received[:half]
        received = exchange(sent, axis, bit)
    return kept + received


def all_sum(value):
    for axis in ("items", "users"):
        for bit in gather_order(lax.axis_size(axis))[::-1]:
            value = value + exchange(value, axis, bit)
    return value


def tiles_kernel(count, source, target, low_ref, high_ref, tile_ref, keep_ref, send_ref, pieces, total, *, transposed):
    step = pl.program_id(0)
    half = low_ref.shape[0]

    @pl.when(step == 0)
    def _():
        def prepare(at, carry):
            for offset, ref in ((0, low_ref), (half, high_ref)):
                value = ref[at]
                top = value.astype(jnp.bfloat16)
                pieces[offset + at, :K] = top
                pieces[offset + at, K:] = (value - top.astype(jnp.float32)).astype(jnp.bfloat16)
                total[offset + at] = jnp.zeros((2 * K, TILE), jnp.float32)
            return carry

        lax.fori_loop(0, half, prepare, 0, unroll=4)

    live = jnp.clip(count[0] - step * BATCH, 0, BATCH)
    contract = 1 if transposed else 0

    def group(at, carry):
        first = at * UNROLL
        products = []
        for slot in range(UNROLL):
            products.append(
                lax.dot_general(
                    pieces[source[step * BATCH + first + slot]],
                    tile_ref[first + slot],
                    (((1,), (contract,)), ((), ())),
                    preferred_element_type=jnp.float32,
                )
            )
        for slot in range(UNROLL):
            total[target[step * BATCH + first + slot]] += products[slot]
        return carry

    lax.fori_loop(0, (live + UNROLL - 1) // UNROLL, group, 0)

    @pl.when(step == pl.num_programs(0) - 1)
    def _():
        def finish(at, carry):
            for offset, ref in ((0, keep_ref), (half, send_ref)):
                ref[at] = total[offset + at, :K] + total[offset + at, K:]
            return carry

        lax.fori_loop(0, half, finish, 0, unroll=4)


def tiles_product(count, source, target, low, high, tiles, blocks_out, transposed):
    half_in = low.shape[0]
    half_out = blocks_out // 2
    whole = lambda step, *refs: (0, 0, 0)

    def tile_block(step, count, source, target):
        return (jnp.minimum(step, (count[0] + BATCH - 1) // BATCH - 1), 0, 0)

    return pl.pallas_call(
        functools.partial(tiles_kernel, transposed=transposed),
        out_shape=[jax.ShapeDtypeStruct((half_out, K, TILE), jnp.float32)] * 2,
        grid_spec=pltpu.PrefetchScalarGridSpec(
            num_scalar_prefetch=3,
            grid=(tiles.shape[0] // BATCH,),
            in_specs=[
                pl.BlockSpec((half_in, K, TILE), whole),
                pl.BlockSpec((half_in, K, TILE), whole),
                pl.BlockSpec((BATCH, TILE, TILE), tile_block),
            ],
            out_specs=[pl.BlockSpec((half_out, K, TILE), whole)] * 2,
            scratch_shapes=[
                pltpu.VMEM((2 * half_in, 2 * K, TILE), jnp.bfloat16),
                pltpu.VMEM((2 * half_out + 1, 2 * K, TILE), jnp.float32),
            ],
        ),
        name="user_tiles" if transposed else "item_tiles",
    )(count, source, target, low, high, tiles)


def dot_full(left, right, contract):
    return lax.dot_general(
        left, right, ((contract[:1], contract[1:]), ((), ())), precision=HIGHEST, preferred_element_type=jnp.float32
    )


def scale_kernel(inverse_ref, raw_ref, scale_ref, panel_ref, sent_ref, gram_ref):
    gram = jnp.zeros((K, K), jnp.float32)
    for at in range(raw_ref.shape[0]):
        scale = scale_ref[at][None, :]
        panel = raw_ref[at]
        if inverse_ref is not None:
            panel = dot_full(inverse_ref[...], panel, (1, 0))
        panel = scale * panel
        panel_ref[at] = panel
        sent_ref[at] = scale * panel
        gram = gram + dot_full(panel, panel, (1, 1))
    gram_ref[...] = gram


def scale_panel(inverse, raw, scale):
    kernel = scale_kernel if inverse is not None else functools.partial(scale_kernel, None)
    operands = (raw, scale) if inverse is None else (inverse, raw, scale)
    shape = jax.ShapeDtypeStruct(raw.shape, jnp.float32)
    return pl.pallas_call(
        kernel,
        out_shape=[shape, shape, jax.ShapeDtypeStruct((K, K), jnp.float32)],
        name="scale_panel",
    )(*operands)


def finish_kernel(inverse_ref, panel_ref, out_ref):
    for at in range(panel_ref.shape[0]):
        out_ref[:, at * TILE : (at + 1) * TILE] = dot_full(inverse_ref[...], panel_ref[at], (1, 0))


def finish_panel(inverse, panel):
    return pl.pallas_call(
        finish_kernel,
        out_shape=jax.ShapeDtypeStruct((K, panel.shape[0] * TILE), jnp.float32),
        name="finish_panel",
    )(inverse, panel)


def inverse_factor(gram, total):
    lower = jnp.linalg.cholesky(gram / total)
    return lax.linalg.triangular_solve(lower, jnp.eye(K, dtype=jnp.float32), left_side=True, lower=True)


def body(tile_rows, tile_cols, tile_count, tile_vals, user_degree, item_degree, start_items):
    user_groups = lax.axis_size("users")
    item_groups = lax.axis_size("items")
    user_blocks = UT // item_groups
    item_blocks = IT // user_groups
    user_total = UT * TILE * user_groups
    item_total = IT * TILE * item_groups

    rows = tile_rows[0, 0]
    cols = tile_cols[0, 0]
    tiles = tile_vals[0, 0]
    count = tile_count[0]
    live = jnp.arange(rows.shape[0], dtype=jnp.int32) < count[0]
    row_place = relative_position(rows // user_blocks, "items") * user_blocks + rows % user_blocks
    col_place = relative_position(cols // item_blocks, "users") * item_blocks + cols % item_blocks
    row_target = jnp.where(live, row_place, UT)
    col_target = jnp.where(live, col_place, IT)

    user_scale = lax.rsqrt(user_degree.astype(jnp.float32)).reshape(user_blocks, TILE)
    item_scale = lax.rsqrt(item_degree.astype(jnp.float32)).reshape(item_blocks, TILE)
    start = start_items.astype(jnp.float32).reshape(K, item_blocks, TILE).transpose(1, 0, 2)
    sent_items = item_scale[:, None, :] * start
    item_inverse = None
    for step in range(ITERS):
        low, high = all_gather_halves(sent_items, "users")
        kept, sent = tiles_product(count, col_place, row_target, low, high, tiles, UT, True)
        user_sum = reduce_scatter_halves(kept, sent, "items")
        user_raw, sent_users, user_gram = scale_panel(item_inverse, user_sum, user_scale)

        low, high = all_gather_halves(sent_users, "items")
        user_inverse = inverse_factor(all_sum(user_gram), user_total)
        kept, sent = tiles_product(count, row_place, col_target, low, high, tiles, IT, False)
        item_sum = reduce_scatter_halves(kept, sent, "users")
        item_raw, sent_items, item_gram = scale_panel(user_inverse, item_sum, item_scale)
        item_inverse = inverse_factor(all_sum(item_gram), item_total)
    return finish_panel(user_inverse, user_raw), finish_panel(item_inverse, item_raw)


def solution(mesh):
    in_specs = (
        P("users", "items", None),
        P("users", "items", None),
        P("users", "items"),
        P("users", "items", None, None, None),
        P(("users", "items")),
        P(("items", "users")),
        P(None, ("items", "users")),
    )
    out_specs = (P(None, ("users", "items")), P(None, ("items", "users")))
    return jax.shard_map(body, mesh=mesh, in_specs=in_specs, out_specs=out_specs, check_vma=False)
```

```python
import functools

import jax
import jax.numpy as jnp
from jax import lax
from jax.experimental import pallas as pl
from jax.experimental.pallas import tpu as pltpu
from jax.sharding import PartitionSpec as P

K = 64
PARTS = 2
ROWS = K // PARTS
TILE = 128
ITERS = 2
UT = 64
IT = 64
BATCH = 64
UNROLL = 64
HIGHEST = lax.Precision.HIGHEST


def gather_order(axis, part):
    order = []
    bit = lax.axis_size(axis) >> 1
    while bit:
        order.append(bit)
        bit >>= 1
    if axis == "users" and part == 1:
        order[-2:] = order[-2:][::-1]
    return order


def exchange(value, axis, bit):
    return lax.ppermute(value, axis, [(at, at ^ bit) for at in range(lax.axis_size(axis))])


def relative_position(shard, axis, part):
    apart = shard ^ lax.axis_index(axis)
    place = jnp.zeros_like(apart)
    for level, bit in enumerate(gather_order(axis, part)):
        place = place + jnp.where(apart & bit != 0, 1 << level, 0)
    return place


def gather(held, axis, part):
    order = gather_order(axis, part)
    for bit in order[:-1]:
        got = exchange(held, axis, bit)
        held = jnp.concatenate([held[:-1], got[:-1], held[-1:] + got[-1:]], axis=0)
    return held, exchange(held, axis, order[-1])


def reduce_scatter(kept, sent, axis, part):
    order = gather_order(axis, part)[::-1]
    got = exchange(sent, axis, order[0])
    for bit in order[1:]:
        half = kept.shape[0] // 2
        sent = kept[half:] + got[half:]
        kept, got = kept[:half], got[:half]
        gram = sent[-1:]
        kept = jnp.concatenate([kept + got, gram], axis=0)
        got = exchange(sent, axis, bit)
    return kept + got


def all_sum(value):
    for axis in ("items", "users"):
        for bit in gather_order(axis, 0)[::-1]:
            value = value + exchange(value, axis, bit)
    return value


def tiles_kernel(count, source, target, low_ref, high_ref, tile_ref, keep_ref, send_ref, pieces, total, *, transposed):
    step = pl.program_id(0)
    half_in = low_ref.shape[0] - 1
    half_out = keep_ref.shape[0] - 1

    @pl.when(step == 0)
    def _():
        def prepare(at, carry):
            for offset, ref in ((0, low_ref), (half_in, high_ref)):
                value = ref[at]
                top = value.astype(jnp.bfloat16)
                pieces[offset + at, :ROWS] = top
                pieces[offset + at, ROWS:] = (value - top.astype(jnp.float32)).astype(jnp.bfloat16)
            return carry

        def clear(at, carry):
            for offset in (0, half_out):
                total[offset + at] = jnp.zeros((2 * ROWS, TILE), jnp.float32)
            return carry

        lax.fori_loop(0, half_in, prepare, 0, unroll=4)
        lax.fori_loop(0, half_out, clear, 0, unroll=4)

    live = jnp.clip(count[0] - step * BATCH, 0, BATCH)
    contract = 1 if transposed else 0

    def group(at, carry):
        first = at * UNROLL
        products = []
        for slot in range(UNROLL):
            products.append(
                lax.dot_general(
                    pieces[source[step * BATCH + first + slot]],
                    tile_ref[first + slot],
                    (((1,), (contract,)), ((), ())),
                    preferred_element_type=jnp.float32,
                )
            )
        for slot in range(UNROLL):
            total[target[step * BATCH + first + slot]] += products[slot]
        return carry

    lax.fori_loop(0, (live + UNROLL - 1) // UNROLL, group, 0)

    @pl.when(step == pl.num_programs(0) - 1)
    def _():
        def finish(at, carry):
            for offset, ref in ((0, keep_ref), (half_out, send_ref)):
                ref[at] = total[offset + at, :ROWS] + total[offset + at, ROWS:]
            return carry

        lax.fori_loop(0, half_out, finish, 0, unroll=4)
        gram = low_ref[half_in] + high_ref[half_in]
        keep_ref[half_out] = gram
        send_ref[half_out] = gram


def tiles_product(count, source, target, low, high, tiles, blocks_out, transposed):
    half_in = low.shape[0] - 1
    half_out = blocks_out // 2
    whole = lambda step, *refs: (0, 0, 0)

    def tile_block(step, count, source, target):
        return (jnp.minimum(step, (count[0] + BATCH - 1) // BATCH - 1), 0, 0)

    return pl.pallas_call(
        functools.partial(tiles_kernel, transposed=transposed),
        out_shape=[jax.ShapeDtypeStruct((half_out + 1, ROWS, TILE), jnp.float32)] * 2,
        grid_spec=pltpu.PrefetchScalarGridSpec(
            num_scalar_prefetch=3,
            grid=(tiles.shape[0] // BATCH,),
            in_specs=[
                pl.BlockSpec((half_in + 1, ROWS, TILE), whole),
                pl.BlockSpec((half_in + 1, ROWS, TILE), whole),
                pl.BlockSpec((BATCH, TILE, TILE), tile_block),
            ],
            out_specs=[pl.BlockSpec((half_out + 1, ROWS, TILE), whole)] * 2,
            scratch_shapes=[
                pltpu.VMEM((2 * half_in, 2 * ROWS, TILE), jnp.bfloat16),
                pltpu.VMEM((2 * half_out + 1, 2 * ROWS, TILE), jnp.float32),
            ],
        ),
        name="user_tiles" if transposed else "item_tiles",
    )(count, source, target, low, high, tiles)


def dot_full(left, right, contract):
    return lax.dot_general(
        left, right, ((contract[:1], contract[1:]), ((), ())), precision=HIGHEST, preferred_element_type=jnp.float32
    )


def inverse_factor(gram):
    size = gram.shape[0]
    row = lax.broadcasted_iota(jnp.int32, (size, size), 0)
    col = lax.broadcasted_iota(jnp.int32, (size, size), 1)
    work = jnp.concatenate([gram, (row == col).astype(jnp.float32)], axis=1)
    below = lax.broadcasted_iota(jnp.int32, (size, 1), 0)
    for at in range(size):
        pivot_row = work[at : at + 1, :]
        factor = work[:, at : at + 1] / pivot_row[:, at : at + 1]
        work = work - jnp.where(below > at, factor, 0.0) * pivot_row
    pivots = jnp.sum(jnp.where(row == col, work[:, :size], 0.0), axis=1, keepdims=True)
    return work[:, size:] * lax.rsqrt(pivots)


def apply_factor(solved, raw_refs, at, part):
    if solved is None:
        return raw_refs[part][at]
    if part == 0:
        return dot_full(solved[0], raw_refs[0][at], (1, 0))
    return dot_full(solved[1], raw_refs[1][at] - dot_full(solved[0], raw_refs[0][at], (1, 0)), (1, 0))


def pad_lanes(value):
    return jnp.concatenate([value, jnp.zeros((value.shape[0], TILE - value.shape[1]), jnp.float32)], axis=1)


def scale_kernel(*refs, part, factored, total):
    refs = list(refs)
    raw_refs = [refs.pop(0) for _ in range(part + 1)]
    scale_ref = refs.pop(0)
    other_ref = refs.pop(0) if part else None
    before_ref = refs.pop(0) if part and factored else None
    panel_ref = refs.pop(0)
    sent_ref = refs.pop(0)
    solved = None
    blocks = scale_ref.shape[0]
    if factored:
        gram = raw_refs[part][blocks] * (1.0 / total)
        if part == 0:
            solved = (inverse_factor(gram[:, :ROWS]),)
        else:
            before = before_ref[...]
            lower = dot_full(gram[:, :ROWS], before, (1, 1))
            rest = gram[:, ROWS:K] - dot_full(lower, lower, (1, 1))
            solved = (dot_full(lower, before, (1, 0)), inverse_factor(rest))
        for out_ref, value in zip(refs, solved):
            out_ref[...] = value
    grams = [jnp.zeros((ROWS, ROWS), jnp.float32) for _ in range(part + 1)]
    for at in range(blocks):
        scale = scale_ref[at][None, :]
        panel = scale * apply_factor(solved, raw_refs, at, part)
        panel_ref[at] = panel
        sent_ref[at] = scale * panel
        if part:
            grams[0] = grams[0] + dot_full(panel, other_ref[at], (1, 1))
        grams[part] = grams[part] + dot_full(panel, panel, (1, 1))
    sent_ref[blocks] = pad_lanes(jnp.concatenate(grams, axis=1))


def scale_panel(raws, scale, other, before, part, factored, total):
    operands = list(raws[: part + 1]) + [scale]
    if part:
        operands.append(other)
        if factored:
            operands.append(before)
    blocks = scale.shape[0]
    square = jax.ShapeDtypeStruct((ROWS, ROWS), jnp.float32)
    return pl.pallas_call(
        functools.partial(scale_kernel, part=part, factored=factored, total=total),
        out_shape=[
            jax.ShapeDtypeStruct((blocks, ROWS, TILE), jnp.float32),
            jax.ShapeDtypeStruct((blocks + 1, ROWS, TILE), jnp.float32),
        ]
        + [square] * ((part + 1) if factored else 0),
        name="scale_panel",
    )(*operands)


def finish_kernel(*refs, factored, total):
    raw_refs, rest = refs[:PARTS], refs[PARTS:-1]
    out_ref = refs[-1]
    if factored:
        first, (cross, second) = rest[0][...], (rest[1][...], rest[2][...])
    else:
        gram = rest[0][...] * (1.0 / total)
        first = inverse_factor(gram[:ROWS, :ROWS])
        lower = dot_full(gram[ROWS:, :ROWS], first, (1, 1))
        second = inverse_factor(gram[ROWS:, ROWS:K] - dot_full(lower, lower, (1, 1)))
        cross = dot_full(lower, first, (1, 0))
    for at in range(raw_refs[0].shape[0]):
        lanes = slice(at * TILE, (at + 1) * TILE)
        out_ref[:ROWS, lanes] = apply_factor((first,), raw_refs, at, 0)
        out_ref[ROWS:, lanes] = apply_factor((cross, second), raw_refs, at, 1)


def finish_panel(panels, rest, factored, total):
    return pl.pallas_call(
        functools.partial(finish_kernel, factored=factored, total=total),
        out_shape=jax.ShapeDtypeStruct((K, panels[0].shape[0] * TILE), jnp.float32),
        name="finish_panel",
    )(*panels, *rest)


def body(tile_rows, tile_cols, tile_count, tile_vals, user_degree, item_degree, start_items):
    user_groups = lax.axis_size("users")
    item_groups = lax.axis_size("items")
    user_blocks = UT // item_groups
    item_blocks = IT // user_groups
    user_total = UT * TILE * user_groups
    item_total = IT * TILE * item_groups

    rows = tile_rows[0, 0]
    cols = tile_cols[0, 0]
    tiles = tile_vals[0, 0]
    count = tile_count[0]
    live = jnp.arange(rows.shape[0], dtype=jnp.int32) < count[0]
    row_at, row_to, col_at, col_to = [], [], [], []
    for part in range(PARTS):
        place = relative_position(rows // user_blocks, "items", part) * user_blocks + rows % user_blocks
        row_at.append(place)
        row_to.append(jnp.where(live, place, UT))
        place = relative_position(cols // item_blocks, "users", part) * item_blocks + cols % item_blocks
        col_at.append(place)
        col_to.append(jnp.where(live, place, IT))

    user_scale = lax.rsqrt(user_degree.astype(jnp.float32)).reshape(user_blocks, TILE)
    item_scale = lax.rsqrt(item_degree.astype(jnp.float32)).reshape(item_blocks, TILE)
    start = start_items.astype(jnp.float32).reshape(PARTS, ROWS, item_blocks, TILE).transpose(0, 2, 1, 3)
    start = item_scale[None, :, None, :] * start
    start = jnp.concatenate([start, jnp.zeros_like(start[:, :1])], axis=1)
    sent = [start[part] for part in range(PARTS)]

    def user_half(sent, part):
        low, high = gather(sent, "users", part)
        kept, out = tiles_product(count, col_at[part], row_to[part], low, high, tiles, UT, True)
        return reduce_scatter(kept, out, "items", part)

    def item_half(sent, part):
        low, high = gather(sent, "items", part)
        kept, out = tiles_product(count, row_at[part], col_to[part], low, high, tiles, IT, False)
        return reduce_scatter(kept, out, "users", part)

    def scaled(raws, scale, factored, total):
        first, sent_first, *solved_first = scale_panel(raws, scale, None, None, 0, factored, total)
        before = solved_first[0] if factored else None
        second, sent_second, *solved_second = scale_panel(raws, scale, first, before, 1, factored, total)
        return [first, second], [sent_first, sent_second], solved_first + solved_second

    for step in range(ITERS):
        raws = [user_half(sent[part], part) for part in range(PARTS)]
        user_raw, sent, _ = scaled(raws, user_scale, step > 0, item_total)
        raws = [item_half(sent[part], part) for part in range(PARTS)]
        item_raw, sent, solved = scaled(raws, item_scale, True, user_total)
    gram = all_sum(jnp.concatenate([part[-1] for part in sent], axis=0))
    return finish_panel(user_raw, solved, True, user_total), finish_panel(item_raw, [gram], False, item_total)


def solution(mesh):
    in_specs = (
        P("users", "items", None),
        P("users", "items", None),
        P("users", "items"),
        P("users", "items", None, None, None),
        P(("users", "items")),
        P(("items", "users")),
        P(None, ("items", "users")),
    )
    out_specs = (P(None, ("users", "items")), P(None, ("items", "users")))
    return jax.shard_map(body, mesh=mesh, in_specs=in_specs, out_specs=out_specs, check_vma=False)
```

```python
import functools

import jax
import jax.numpy as jnp
from jax import lax
from jax.experimental import pallas as pl
from jax.experimental.pallas import tpu as pltpu
from jax.sharding import PartitionSpec as P

K = 64
PARTS = 2
ROWS = K // PARTS
TILE = 128
ITERS = 2
UT = 64
IT = 64
BATCH = 64
UNROLL = 64
HIGHEST = lax.Precision.HIGHEST


def gather_order(axis, part):
    order = []
    bit = lax.axis_size(axis) >> 1
    while bit:
        order.append(bit)
        bit >>= 1
    if axis == "users" and part == 1:
        order[-2:] = order[-2:][::-1]
    return order


def exchange(value, axis, bit):
    return lax.ppermute(value, axis, [(at, at ^ bit) for at in range(lax.axis_size(axis))])


def relative_position(shard, axis, part):
    apart = shard ^ lax.axis_index(axis)
    place = jnp.zeros_like(apart)
    for level, bit in enumerate(gather_order(axis, part)):
        place = place + jnp.where(apart & bit != 0, 1 << level, 0)
    return place


def gather(held, axis):
    levels = len(gather_order(axis, 0))
    for level in range(levels - 1):
        got = [exchange(held[part], axis, gather_order(axis, part)[level]) for part in range(PARTS)]
        held = [
            jnp.concatenate([have[:-1], more[:-1], have[-1:] + more[-1:]], axis=0) for have, more in zip(held, got)
        ]
    got = [exchange(held[part], axis, gather_order(axis, part)[-1]) for part in range(PARTS)]
    return held, got


def reduce_scatter(kept, sent, axis):
    levels = len(gather_order(axis, 0))
    for level in range(levels - 1, 0, -1):
        got = [exchange(sent[part], axis, gather_order(axis, part)[level]) for part in range(PARTS)]
        half = kept[0].shape[0] // 2
        sent = [have[half:] + more[half:] for have, more in zip(kept, got)]
        if level > 1:
            kept = [
                jnp.concatenate([have[:half] + more[:half], out[-1:]], axis=0)
                for have, more, out in zip(kept, got, sent)
            ]
        else:
            kept = [have[:half] + more[:half] for have, more in zip(kept, got)]
    bit = gather_order(axis, 0)[0]
    gram = jnp.concatenate([out[-1] for out in sent], axis=0)
    gram = gram + exchange(gram, axis, bit)
    got = [exchange(out[:-1], axis, bit) for out in sent]
    return [have + more for have, more in zip(kept, got)], gram


def all_sum(value):
    for axis in ("items", "users"):
        for bit in gather_order(axis, 0)[::-1]:
            value = value + exchange(value, axis, bit)
    return value


def part_places(axis, part, blocks):
    swapped = gather_order(axis, part) != gather_order(axis, 0)
    quarter = blocks // 4
    return [at * quarter for at in ((0, 2, 1, 3) if swapped else (0, 1, 2, 3))], quarter


def tiles_kernel(count, source, target, *refs, transposed, places_in, places_out):
    low_refs, high_refs, refs = refs[:PARTS], refs[PARTS : 2 * PARTS], refs[2 * PARTS :]
    tile_ref, keep_refs, send_refs = refs[0], refs[1 : 1 + PARTS], refs[1 + PARTS : 1 + 2 * PARTS]
    pieces, total = refs[1 + 2 * PARTS :]
    step = pl.program_id(0)
    half_in = low_refs[0].shape[0] - 1
    half_out = keep_refs[0].shape[0] - 1

    @pl.when(step == 0)
    def _():
        for part in range(PARTS):
            starts, quarter = places_in[part]
            band = slice(part * ROWS, (part + 1) * ROWS)
            for at, place in enumerate(starts):
                ref = (low_refs, low_refs, high_refs, high_refs)[at][part]
                first = at % 2 * quarter

                def prepare(block, carry):
                    value = ref[first + block]
                    top = value.astype(jnp.bfloat16)
                    pieces[place + block, band, :TILE] = top
                    pieces[place + block, band, TILE:] = (value - top.astype(jnp.float32)).astype(jnp.bfloat16)
                    return carry

                lax.fori_loop(0, quarter, prepare, 0, unroll=4)

        def clear(at, carry):
            total[at] = jnp.zeros((K, TILE), jnp.float32)
            return carry

        lax.fori_loop(0, 2 * half_out, clear, 0, unroll=4)

    live = jnp.clip(count[0] - step * BATCH, 0, BATCH)
    contract = 1 if transposed else 0

    def group(at, carry):
        first = at * UNROLL
        products = []
        for slot in range(UNROLL):
            tile = tile_ref[first + slot]
            products.append(
                lax.dot_general(
                    pieces[source[step * BATCH + first + slot]],
                    jnp.concatenate([tile, tile], axis=contract),
                    (((1,), (contract,)), ((), ())),
                    preferred_element_type=jnp.float32,
                )
            )
        for slot in range(UNROLL):
            total[target[step * BATCH + first + slot]] += products[slot]
        return carry

    lax.fori_loop(0, (live + UNROLL - 1) // UNROLL, group, 0)

    @pl.when(step == pl.num_programs(0) - 1)
    def _():
        for part in range(PARTS):
            starts, quarter = places_out[part]
            band = slice(part * ROWS, (part + 1) * ROWS)
            for at, place in enumerate(starts):
                ref = (keep_refs, keep_refs, send_refs, send_refs)[at][part]
                first = at % 2 * quarter

                def finish(block, carry):
                    ref[first + block] = total[place + block, band]
                    return carry

                lax.fori_loop(0, quarter, finish, 0, unroll=4)
            gram = low_refs[part][half_in] + high_refs[part][half_in]
            keep_refs[part][half_out] = gram
            send_refs[part][half_out] = gram


def tiles_product(count, source, target, low, high, tiles, blocks_out, axis_in, axis_out, transposed):
    half_in = low[0].shape[0] - 1
    half_out = blocks_out // 2
    whole = lambda step, *refs: (0, 0, 0)

    def tile_block(step, count, source, target):
        return (jnp.minimum(step, (count[0] + BATCH - 1) // BATCH - 1), 0, 0)

    kernel = functools.partial(
        tiles_kernel,
        transposed=transposed,
        places_in=[part_places(axis_in, part, 2 * half_in) for part in range(PARTS)],
        places_out=[part_places(axis_out, part, 2 * half_out) for part in range(PARTS)],
    )
    out = pl.pallas_call(
        kernel,
        out_shape=[jax.ShapeDtypeStruct((half_out + 1, ROWS, TILE), jnp.float32)] * (2 * PARTS),
        grid_spec=pltpu.PrefetchScalarGridSpec(
            num_scalar_prefetch=3,
            grid=(tiles.shape[0] // BATCH,),
            in_specs=[pl.BlockSpec((half_in + 1, ROWS, TILE), whole)] * (2 * PARTS)
            + [pl.BlockSpec((BATCH, TILE, TILE), tile_block)],
            out_specs=[pl.BlockSpec((half_out + 1, ROWS, TILE), whole)] * (2 * PARTS),
            scratch_shapes=[
                pltpu.VMEM((2 * half_in, K, 2 * TILE), jnp.bfloat16),
                pltpu.VMEM((2 * half_out + 1, K, TILE), jnp.float32),
            ],
        ),
        name="user_tiles" if transposed else "item_tiles",
    )(count, source, target, *low, *high, tiles)
    return out[:PARTS], out[PARTS:]


def dot_full(left, right, contract):
    return lax.dot_general(
        left, right, ((contract[:1], contract[1:]), ((), ())), precision=HIGHEST, preferred_element_type=jnp.float32
    )


def factor_kernel(gram_ref, out_ref, *, total):
    row = lax.broadcasted_iota(jnp.int32, (K, K), 0)
    col = lax.broadcasted_iota(jnp.int32, (K, K), 1)
    work = jnp.concatenate([gram_ref[:, :K] * (1.0 / total), (row == col).astype(jnp.float32)], axis=1)
    below = lax.broadcasted_iota(jnp.int32, (K, 1), 0)
    for at in range(K):
        pivot_row = work[at : at + 1, :]
        factor = work[:, at : at + 1] / pivot_row[:, at : at + 1]
        work = work - jnp.where(below > at, factor, 0.0) * pivot_row
    pivots = jnp.sum(jnp.where(row == col, work[:, :K], 0.0), axis=1, keepdims=True)
    out_ref[...] = work[:, K:] * lax.rsqrt(pivots)


def inverse_factor(gram, total):
    return pl.pallas_call(
        functools.partial(factor_kernel, total=total),
        out_shape=jax.ShapeDtypeStruct((K, K), jnp.float32),
        name="factor",
    )(gram)


def scale_kernel(*refs, factored):
    refs = list(refs)
    inverse = refs.pop(0)[...] if factored else None
    raw_refs, refs = refs[:PARTS], refs[PARTS:]
    scale_ref, panel_ref, sent_refs = refs[0], refs[1], refs[2:]
    blocks = scale_ref.shape[0]
    gram = jnp.zeros((K, K), jnp.float32)
    for at in range(blocks):
        scale = scale_ref[at][None, :]
        panel = jnp.concatenate([ref[at] for ref in raw_refs], axis=0)
        if factored:
            panel = dot_full(inverse, panel, (1, 0))
        panel = scale * panel
        panel_ref[at] = panel
        for part in range(PARTS):
            sent_refs[part][at] = scale * panel[part * ROWS : (part + 1) * ROWS]
        gram = gram + dot_full(panel, panel, (1, 1))
    gram = jnp.concatenate([gram, jnp.zeros((K, TILE - K), jnp.float32)], axis=1)
    for part in range(PARTS):
        sent_refs[part][blocks] = gram[part * ROWS : (part + 1) * ROWS]


def scale_panel(inverse, raws, scale):
    factored = inverse is not None
    operands = ([inverse] if factored else []) + list(raws) + [scale]
    blocks = scale.shape[0]
    panel, *sent = pl.pallas_call(
        functools.partial(scale_kernel, factored=factored),
        out_shape=[jax.ShapeDtypeStruct((blocks, K, TILE), jnp.float32)]
        + [jax.ShapeDtypeStruct((blocks + 1, ROWS, TILE), jnp.float32)] * PARTS,
        name="scale_panel",
    )(*operands)
    return panel, sent


def finish_kernel(inverse_ref, panel_ref, out_ref):
    for at in range(panel_ref.shape[0]):
        out_ref[:, at * TILE : (at + 1) * TILE] = dot_full(inverse_ref[...], panel_ref[at], (1, 0))


def finish_panel(inverse, panel):
    return pl.pallas_call(
        finish_kernel,
        out_shape=jax.ShapeDtypeStruct((K, panel.shape[0] * TILE), jnp.float32),
        name="finish_panel",
    )(inverse, panel)


def body(tile_rows, tile_cols, tile_count, tile_vals, user_degree, item_degree, start_items):
    user_groups = lax.axis_size("users")
    item_groups = lax.axis_size("items")
    user_blocks = UT // item_groups
    item_blocks = IT // user_groups
    user_total = UT * TILE * user_groups
    item_total = IT * TILE * item_groups

    rows = tile_rows[0, 0]
    cols = tile_cols[0, 0]
    tiles = tile_vals[0, 0]
    count = tile_count[0]
    live = jnp.arange(rows.shape[0], dtype=jnp.int32) < count[0]
    row_at = relative_position(rows // user_blocks, "items", 0) * user_blocks + rows % user_blocks
    col_at = relative_position(cols // item_blocks, "users", 0) * item_blocks + cols % item_blocks
    row_to = jnp.where(live, row_at, UT)
    col_to = jnp.where(live, col_at, IT)

    user_scale = lax.rsqrt(user_degree.astype(jnp.float32)).reshape(user_blocks, TILE)
    item_scale = lax.rsqrt(item_degree.astype(jnp.float32)).reshape(item_blocks, TILE)
    start = start_items.astype(jnp.float32).reshape(PARTS, ROWS, item_blocks, TILE).transpose(0, 2, 1, 3)
    start = item_scale[None, :, None, :] * start
    start = jnp.concatenate([start, jnp.zeros_like(start[:, :1])], axis=1)
    sent = [start[part] for part in range(PARTS)]

    item_inverse = None
    for step in range(ITERS):
        low, high = gather(sent, "users")
        kept, out = tiles_product(count, col_at, row_to, low, high, tiles, UT, "users", "items", True)
        raws, gram = reduce_scatter(kept, out, "items")
        if step:
            item_inverse = inverse_factor(gram, item_total)
        user_raw, sent = scale_panel(item_inverse, raws, user_scale)
        low, high = gather(sent, "items")
        kept, out = tiles_product(count, row_at, col_to, low, high, tiles, IT, "items", "users", False)
        raws, gram = reduce_scatter(kept, out, "users")
        user_inverse = inverse_factor(gram, user_total)
        item_raw, sent = scale_panel(user_inverse, raws, item_scale)
    gram = all_sum(jnp.concatenate([part[-1] for part in sent], axis=0))
    return finish_panel(user_inverse, user_raw), finish_panel(inverse_factor(gram, item_total), item_raw)


def solution(mesh):
    in_specs = (
        P("users", "items", None),
        P("users", "items", None),
        P("users", "items"),
        P("users", "items", None, None, None),
        P(("users", "items")),
        P(("items", "users")),
        P(None, ("items", "users")),
    )
    out_specs = (P(None, ("users", "items")), P(None, ("items", "users")))
    return jax.shard_map(body, mesh=mesh, in_specs=in_specs, out_specs=out_specs, check_vma=False)
```

```python
import functools

import jax
import jax.numpy as jnp
from jax import lax
from jax.experimental import pallas as pl
from jax.experimental.pallas import tpu as pltpu
from jax.sharding import PartitionSpec as P

K = 64
PARTS = 2
ROWS = K // PARTS
TILE = 128
ITERS = 2
UT = 64
IT = 64
BATCH = 64
UNROLL = 64
HIGHEST = lax.Precision.HIGHEST


def gather_order(axis, part):
    order = []
    bit = lax.axis_size(axis) >> 1
    while bit:
        order.append(bit)
        bit >>= 1
    if axis == "users" and part == 1:
        order[-2:] = order[-2:][::-1]
    return order


def exchange(value, axis, bit):
    return lax.ppermute(value, axis, [(at, at ^ bit) for at in range(lax.axis_size(axis))])


def relative_position(shard, axis, part):
    apart = shard ^ lax.axis_index(axis)
    place = jnp.zeros_like(apart)
    for level, bit in enumerate(gather_order(axis, part)):
        place = place + jnp.where(apart & bit != 0, 1 << level, 0)
    return place


def gather(held, axis):
    levels = len(gather_order(axis, 0))
    for level in range(levels - 1):
        got = [exchange(held[part], axis, gather_order(axis, part)[level]) for part in range(PARTS)]
        first = jnp.concatenate([held[0][:-1], got[0][:-1], held[0][-1:] + got[0][-1:]], axis=0)
        held = [first] + [jnp.concatenate([have, more], axis=0) for have, more in zip(held[1:], got[1:])]
    got = [exchange(held[part], axis, gather_order(axis, part)[-1]) for part in range(PARTS)]
    return held, got


def reduce_scatter(kept, sent, axis):
    levels = len(gather_order(axis, 0))
    for level in range(levels - 1, 0, -1):
        got = [exchange(sent[part], axis, gather_order(axis, part)[level]) for part in range(PARTS)]
        half = kept[-1].shape[0] // 2
        if level == 1:
            gram = kept[0][-1] + got[0][-1]
            sent = [have[half : 2 * half] + more[half : 2 * half] for have, more in zip(kept, got)]
            kept = [have[:half] + more[:half] for have, more in zip(kept, got)]
        else:
            sent = [have[half:] + more[half:] for have, more in zip(kept, got)]
            kept = [have[:half] + more[:half] for have, more in zip(kept, got)]
            kept[0] = jnp.concatenate([kept[0], sent[0][-1:]], axis=0)
    bit = gather_order(axis, 0)[0]
    gram = gram + exchange(gram, axis, bit)
    got = [exchange(out, axis, bit) for out in sent]
    return kept, got, gram


def all_sum(value):
    for axis in ("items", "users"):
        for bit in gather_order(axis, 0)[::-1]:
            value = value + exchange(value, axis, bit)
    return value


def part_places(axis, part, blocks):
    swapped = gather_order(axis, part) != gather_order(axis, 0)
    quarter = blocks // 4
    return [at * quarter for at in ((0, 2, 1, 3) if swapped else (0, 1, 2, 3))], quarter


def tiles_kernel(count, source, target, *refs, places_in, places_out):
    low_refs, high_refs, refs = refs[:PARTS], refs[PARTS : 2 * PARTS], refs[2 * PARTS :]
    tile_ref, keep_refs, send_refs = refs[0], refs[1 : 1 + PARTS], refs[1 + PARTS : 1 + 2 * PARTS]
    pieces, total = refs[1 + 2 * PARTS :]
    step = pl.program_id(0)
    half_in = low_refs[-1].shape[0]
    half_out = keep_refs[-1].shape[0]

    @pl.when(step == 0)
    def _():
        for part in range(PARTS):
            starts, quarter = places_in[part]
            band = slice(part * ROWS, (part + 1) * ROWS)
            for at, place in enumerate(starts):
                ref = (low_refs, low_refs, high_refs, high_refs)[at][part]
                first = at % 2 * quarter

                def prepare(block, carry):
                    value = ref[first + block]
                    top = value.astype(jnp.bfloat16)
                    pieces[place + block, band, :TILE] = top
                    pieces[place + block, band, TILE:] = (value - top.astype(jnp.float32)).astype(jnp.bfloat16)
                    return carry

                lax.fori_loop(0, quarter, prepare, 0, unroll=4)

        def clear(at, carry):
            total[at] = jnp.zeros((K, TILE), jnp.float32)
            return carry

        lax.fori_loop(0, 2 * half_out, clear, 0, unroll=4)

    live = jnp.clip(count[0] - step * BATCH, 0, BATCH)

    def group(at, carry):
        first = at * UNROLL
        products = []
        for slot in range(UNROLL):
            tile = tile_ref[first + slot]
            products.append(
                lax.dot_general(
                    pieces[source[step * BATCH + first + slot]],
                    jnp.concatenate([tile, tile], axis=0),
                    (((1,), (0,)), ((), ())),
                    preferred_element_type=jnp.float32,
                )
            )
        for slot in range(UNROLL):
            total[target[step * BATCH + first + slot]] += products[slot]
        return carry

    lax.fori_loop(0, (live + UNROLL - 1) // UNROLL, group, 0)

    @pl.when(step == pl.num_programs(0) - 1)
    def _():
        for part in range(PARTS):
            starts, quarter = places_out[part]
            band = slice(part * ROWS, (part + 1) * ROWS)
            for at, place in enumerate(starts):
                ref = (keep_refs, keep_refs, send_refs, send_refs)[at][part]
                first = at % 2 * quarter

                def finish(block, carry):
                    ref[first + block] = total[place + block, band]
                    return carry

                lax.fori_loop(0, quarter, finish, 0, unroll=4)
        gram = low_refs[0][half_in] + high_refs[0][half_in]
        keep_refs[0][half_out] = gram
        send_refs[0][half_out] = gram


def tiles_product(count, source, target, low, high, tiles, blocks_out, axis_in, axis_out):
    half_in = low[-1].shape[0]
    half_out = blocks_out // 2
    whole = lambda step, *refs: (0, 0, 0)
    shapes = lambda blocks: [(blocks + (part == 0), ROWS, TILE) for part in range(PARTS)]

    def tile_block(step, count, source, target):
        return (jnp.minimum(step, (count[0] + BATCH - 1) // BATCH - 1), 0, 0)

    kernel = functools.partial(
        tiles_kernel,
        places_in=[part_places(axis_in, part, 2 * half_in) for part in range(PARTS)],
        places_out=[part_places(axis_out, part, 2 * half_out) for part in range(PARTS)],
    )
    out = pl.pallas_call(
        kernel,
        out_shape=[jax.ShapeDtypeStruct(shape, jnp.float32) for shape in shapes(half_out)] * 2,
        grid_spec=pltpu.PrefetchScalarGridSpec(
            num_scalar_prefetch=3,
            grid=(tiles.shape[0] // BATCH,),
            in_specs=[pl.BlockSpec(shape, whole) for shape in shapes(half_in)] * 2
            + [pl.BlockSpec((BATCH, TILE, TILE), tile_block)],
            out_specs=[pl.BlockSpec(shape, whole) for shape in shapes(half_out)] * 2,
            scratch_shapes=[
                pltpu.VMEM((2 * half_in, K, 2 * TILE), jnp.bfloat16),
                pltpu.VMEM((2 * half_out + 1, K, TILE), jnp.float32),
            ],
        ),
        name=axis_out + "_tiles",
    )(count, source, target, *low, *high, tiles)
    return out[:PARTS], out[PARTS:]


def dot_full(left, right, contract):
    return lax.dot_general(
        left, right, ((contract[:1], contract[1:]), ((), ())), precision=HIGHEST, preferred_element_type=jnp.float32
    )


def factor_kernel(gram_ref, out_ref, *, total):
    row = lax.broadcasted_iota(jnp.int32, (K, K), 0)
    col = lax.broadcasted_iota(jnp.int32, (K, K), 1)
    gram = jnp.concatenate([gram_ref[:, :K], gram_ref[:, K:]], axis=0) * (1.0 / total)
    work = jnp.concatenate([gram, (row == col).astype(jnp.float32)], axis=1)
    below = lax.broadcasted_iota(jnp.int32, (K, 1), 0)
    for at in range(0, K, 2):
        first, second = work[at : at + 1, :], work[at + 1 : at + 2, :]
        beside = first[:, at + 1 : at + 2]
        inverse = 1.0 / first[:, at : at + 1]
        multiple = beside * inverse
        pivot = second[:, at + 1 : at + 2] - multiple * beside
        second = second - multiple * first
        column = work[:, at : at + 1] * inverse
        next_column = (work[:, at + 1 : at + 2] - column * beside) * (1.0 / pivot)
        work = work - jnp.where(below > at, column, 0.0) * first
        work = work - jnp.where(below > at + 1, next_column, 0.0) * second
    pivots = jnp.sum(jnp.where(row == col, work[:, :K], 0.0), axis=1, keepdims=True)
    out_ref[...] = work[:, K:] * lax.rsqrt(pivots)


def turn_kernel(tile_ref, out_ref):
    for at in range(tile_ref.shape[0]):
        out_ref[at] = tile_ref[at].T


def turned_tiles(tiles):
    block = pl.BlockSpec((32, TILE, TILE), lambda step: (step, 0, 0))
    return pl.pallas_call(
        turn_kernel,
        out_shape=jax.ShapeDtypeStruct(tiles.shape, tiles.dtype),
        grid=(tiles.shape[0] // 32,),
        in_specs=[block],
        out_specs=block,
        name="turned_tiles",
    )(tiles)


def inverse_factor(gram, total):
    return pl.pallas_call(
        functools.partial(factor_kernel, total=total),
        out_shape=jax.ShapeDtypeStruct((K, K), jnp.float32),
        name="factor",
    )(gram)


def scale_kernel(*refs, factored):
    refs = list(refs)
    inverse = refs.pop(0)[...] if factored else None
    raw_refs, refs = list(zip(refs[:PARTS], refs[PARTS : 2 * PARTS])), refs[2 * PARTS :]
    scale_ref, panel_ref, sent_refs = refs[0], refs[1], refs[2:]
    blocks = scale_ref.shape[0]
    gram = jnp.zeros((K, K), jnp.float32)
    for at in range(blocks):
        scale = scale_ref[at][None, :]
        panel = jnp.concatenate([kept[at] + got[at] for kept, got in raw_refs], axis=0)
        if factored:
            panel = dot_full(inverse, panel, (1, 0))
        panel = scale * panel
        panel_ref[at] = panel
        for part in range(PARTS):
            sent_refs[part][at] = scale * panel[part * ROWS : (part + 1) * ROWS]
        gram = gram + dot_full(panel, panel, (1, 1))
    sent_refs[0][blocks] = jnp.concatenate([gram[:ROWS], gram[ROWS:]], axis=1)


def scale_panel(inverse, kept, got, scale):
    factored = inverse is not None
    operands = ([inverse] if factored else []) + list(kept) + list(got) + [scale]
    blocks = scale.shape[0]
    panel, *sent = pl.pallas_call(
        functools.partial(scale_kernel, factored=factored),
        out_shape=[jax.ShapeDtypeStruct((blocks, K, TILE), jnp.float32)]
        + [jax.ShapeDtypeStruct((blocks + (part == 0), ROWS, TILE), jnp.float32) for part in range(PARTS)],
        name="scale_panel",
    )(*operands)
    return panel, sent


def finish_kernel(inverse_ref, panel_ref, out_ref):
    for at in range(panel_ref.shape[0]):
        out_ref[:, at * TILE : (at + 1) * TILE] = dot_full(inverse_ref[...], panel_ref[at], (1, 0))


def finish_panel(inverse, panel):
    return pl.pallas_call(
        finish_kernel,
        out_shape=jax.ShapeDtypeStruct((K, panel.shape[0] * TILE), jnp.float32),
        name="finish_panel",
    )(inverse, panel)


def body(tile_rows, tile_cols, tile_count, tile_vals, user_degree, item_degree, start_items):
    user_groups = lax.axis_size("users")
    item_groups = lax.axis_size("items")
    user_blocks = UT // item_groups
    item_blocks = IT // user_groups
    user_total = UT * TILE * user_groups
    item_total = IT * TILE * item_groups

    rows = tile_rows[0, 0]
    cols = tile_cols[0, 0]
    tiles = tile_vals[0, 0]
    count = tile_count[0]
    live = jnp.arange(rows.shape[0], dtype=jnp.int32) < count[0]
    row_at = relative_position(rows // user_blocks, "items", 0) * user_blocks + rows % user_blocks
    col_at = relative_position(cols // item_blocks, "users", 0) * item_blocks + cols % item_blocks
    row_to = jnp.where(live, row_at, UT)
    col_to = jnp.where(live, col_at, IT)

    user_scale = lax.rsqrt(user_degree.astype(jnp.float32)).reshape(user_blocks, TILE)
    item_scale = lax.rsqrt(item_degree.astype(jnp.float32)).reshape(item_blocks, TILE)
    start = start_items.astype(jnp.float32).reshape(PARTS, ROWS, item_blocks, TILE).transpose(0, 2, 1, 3)
    start = item_scale[None, :, None, :] * start
    sent = [jnp.concatenate([start[0], jnp.zeros_like(start[0][:1])], axis=0), start[1]]
    turned = turned_tiles(tiles)
    item_inverse = None
    for step in range(ITERS):
        low, high = gather(sent, "users")
        kept, out = tiles_product(count, col_at, row_to, low, high, turned, UT, "users", "items")
        kept, got, gram = reduce_scatter(kept, out, "items")
        if step:
            item_inverse = inverse_factor(gram, item_total)
        user_raw, sent = scale_panel(item_inverse, kept, got, user_scale)
        low, high = gather(sent, "items")
        kept, out = tiles_product(count, row_at, col_to, low, high, tiles, IT, "items", "users")
        kept, got, gram = reduce_scatter(kept, out, "users")
        user_inverse = inverse_factor(gram, user_total)
        if step == ITERS - 1:
            user_panel = finish_panel(user_inverse, user_raw)
            user_panel, got = lax.optimization_barrier((user_panel, got))
        item_raw, sent = scale_panel(user_inverse, kept, got, item_scale)
    item_inverse = inverse_factor(all_sum(sent[0][-1]), item_total)
    return user_panel, finish_panel(item_inverse, item_raw)


def solution(mesh):
    in_specs = (
        P("users", "items", None),
        P("users", "items", None),
        P("users", "items"),
        P("users", "items", None, None, None),
        P(("users", "items")),
        P(("items", "users")),
        P(None, ("items", "users")),
    )
    out_specs = (P(None, ("users", "items")), P(None, ("items", "users")))
    return jax.shard_map(body, mesh=mesh, in_specs=in_specs, out_specs=out_specs, check_vma=False)
```

```python
import functools

import jax
import jax.numpy as jnp
from jax import lax
from jax.experimental import pallas as pl
from jax.experimental.pallas import tpu as pltpu
from jax.sharding import PartitionSpec as P


K = 64
PARTS = 2
ROWS = K // PARTS
TILE = 128
ITERS = 2
UT = 64
IT = 64
BATCH = 64
UNROLL = 64
HIGHEST = lax.Precision.HIGHEST
VMEM_SPEC = pl.BlockSpec(memory_space=pltpu.VMEM)


def gather_order(axis, part):
    order = []
    bit = lax.axis_size(axis) >> 1
    while bit:
        order.append(bit)
        bit >>= 1
    if axis == "users" and part == 1:
        order[-2:] = order[-2:][::-1]
    return order


def exchange(value, axis, bit):
    return lax.ppermute(value, axis, [(at, at ^ bit) for at in range(lax.axis_size(axis))])


def relative_position(shard, axis, part):
    apart = shard ^ lax.axis_index(axis)
    place = jnp.zeros_like(apart)
    for level, bit in enumerate(gather_order(axis, part)):
        place = place + jnp.where(apart & bit != 0, 1 << level, 0)
    return place


def gather(held, axis):
    held = list(held)
    levels = len(gather_order(axis, 0))
    for level in range(levels - 2):
        got = [exchange(held[part], axis, gather_order(axis, part)[level]) for part in range(PARTS)]
        first = jnp.concatenate([held[0][:-1], got[0][:-1], held[0][-1:] + got[0][-1:]], axis=0)
        held = [first] + [jnp.concatenate([have, more], axis=0) for have, more in zip(held[1:], got[1:])]
    order = [gather_order(axis, part)[-2:] for part in range(PARTS)]
    near = [exchange(held[part], axis, order[part][0]) for part in range(PARTS)]
    own = [exchange(held[part], axis, order[part][1]) for part in range(PARTS)]
    far = [exchange(near[part], axis, order[part][1]) for part in range(PARTS)]
    return [[held[part], near[part], own[part], far[part]] for part in range(PARTS)]


def reduce_scatter(kept, sent, axis):
    levels = len(gather_order(axis, 0))
    for level in range(levels - 1, 0, -1):
        got = [exchange(sent[part], axis, gather_order(axis, part)[level]) for part in range(PARTS)]
        half = kept[-1].shape[0] // 2
        if level == 1:
            gram = kept[0][-1] + got[0][-1]
            sent = [have[half : 2 * half] + more[half : 2 * half] for have, more in zip(kept, got)]
            kept = [have[:half] + more[:half] for have, more in zip(kept, got)]
        else:
            sent = [have[half:] + more[half:] for have, more in zip(kept, got)]
            kept = [have[:half] + more[:half] for have, more in zip(kept, got)]
            kept[0] = jnp.concatenate([kept[0], sent[0][-1:]], axis=0)
    bit = gather_order(axis, 0)[0]
    gram = gram + exchange(gram, axis, bit)
    got = [exchange(out, axis, bit) for out in sent]
    return kept, got, gram


def all_sum(value):
    for axis in ("items", "users"):
        for bit in gather_order(axis, 0)[::-1]:
            value = value + exchange(value, axis, bit)
    return value


def part_places(axis, part, blocks):
    swapped = gather_order(axis, part) != gather_order(axis, 0)
    quarter = blocks // 4
    return [at * quarter for at in ((0, 2, 1, 3) if swapped else (0, 1, 2, 3))], quarter


def tiles_kernel(count, source, target, *refs, places_in, places_out):
    piece_refs, refs = [refs[4 * part : 4 * part + 4] for part in range(PARTS)], refs[4 * PARTS :]
    tile_ref, keep_refs, send_refs = refs[0], refs[1 : 1 + PARTS], refs[1 + PARTS : 1 + 2 * PARTS]
    pieces, total = refs[1 + 2 * PARTS :]
    step = pl.program_id(0)
    half_out = keep_refs[-1].shape[0]

    @pl.when(step == 0)
    def _():
        for part in range(PARTS):
            starts, quarter = places_in[part]
            band = slice(part * ROWS, (part + 1) * ROWS)
            for at, place in enumerate(starts):
                ref = piece_refs[part][at]

                def prepare(block, carry):
                    value = ref[block]
                    top = value.astype(jnp.bfloat16)
                    pieces[place + block, band, :TILE] = top
                    pieces[place + block, band, TILE:] = (value - top.astype(jnp.float32)).astype(jnp.bfloat16)
                    return carry

                lax.fori_loop(0, quarter, prepare, 0, unroll=4)

        def clear(at, carry):
            total[at] = jnp.zeros((K, TILE), jnp.float32)
            return carry

        lax.fori_loop(0, 2 * half_out, clear, 0, unroll=4)

    live = jnp.clip(count[0] - step * BATCH, 0, BATCH)

    def group(at, carry):
        first = at * UNROLL
        products = []
        for slot in range(UNROLL):
            tile = tile_ref[first + slot]
            products.append(
                lax.dot_general(
                    pieces[source[step * BATCH + first + slot]],
                    jnp.concatenate([tile, tile], axis=0),
                    (((1,), (0,)), ((), ())),
                    preferred_element_type=jnp.float32,
                )
            )
        for slot in range(UNROLL):
            total[target[step * BATCH + first + slot]] += products[slot]
        return carry

    lax.fori_loop(0, (live + UNROLL - 1) // UNROLL, group, 0)

    @pl.when(step == pl.num_programs(0) - 1)
    def _():
        for part in range(PARTS):
            starts, quarter = places_out[part]
            band = slice(part * ROWS, (part + 1) * ROWS)
            for at, place in enumerate(starts):
                ref = (keep_refs, keep_refs, send_refs, send_refs)[at][part]
                first = at % 2 * quarter

                def finish(block, carry):
                    ref[first + block] = total[place + block, band]
                    return carry

                lax.fori_loop(0, quarter, finish, 0, unroll=4)
        near, own = piece_refs[0][0].shape[0] - 1, piece_refs[0][2].shape[0] - 1
        gram = (piece_refs[0][0][near] + piece_refs[0][1][near]) + (piece_refs[0][2][own] + piece_refs[0][3][own])
        keep_refs[0][half_out] = gram
        send_refs[0][half_out] = gram


def tiles_product(count, source, target, pieces, tiles, blocks_out, axis_in, axis_out):
    quarter_in = pieces[-1][0].shape[0]
    half_out = blocks_out // 2
    shapes = lambda blocks: [(blocks + (part == 0), ROWS, TILE) for part in range(PARTS)]

    def tile_block(step, count, source, target):
        return (jnp.minimum(step, (count[0] + BATCH - 1) // BATCH - 1), 0, 0)

    kernel = functools.partial(
        tiles_kernel,
        places_in=[part_places(axis_in, part, 4 * quarter_in) for part in range(PARTS)],
        places_out=[part_places(axis_out, part, 2 * half_out) for part in range(PARTS)],
    )
    out = pl.pallas_call(
        kernel,
        out_shape=[jax.ShapeDtypeStruct(shape, jnp.float32) for shape in shapes(half_out)] * 2,
        grid_spec=pltpu.PrefetchScalarGridSpec(
            num_scalar_prefetch=3,
            grid=(tiles.shape[0] // BATCH,),
            in_specs=[VMEM_SPEC] * (4 * PARTS)
            + [pl.BlockSpec((BATCH, TILE, TILE), tile_block)],
            out_specs=[VMEM_SPEC] * (2 * PARTS),
            scratch_shapes=[
                pltpu.VMEM((4 * quarter_in, K, 2 * TILE), jnp.bfloat16),
                pltpu.VMEM((2 * half_out + 1, K, TILE), jnp.float32),
            ],
        ),
    )(count, source, target, *pieces[0], *pieces[1], tiles)
    return out[:PARTS], out[PARTS:]


def dot_full(left, right, contract):
    return lax.dot_general(
        left, right, ((contract[:1], contract[1:]), ((), ())), precision=HIGHEST, preferred_element_type=jnp.float32
    )


def factor_kernel(gram_ref, out_ref, *, total):
    row = lax.broadcasted_iota(jnp.int32, (K, K), 0)
    col = lax.broadcasted_iota(jnp.int32, (K, K), 1)
    gram = jnp.concatenate([gram_ref[:, :K], gram_ref[:, K:]], axis=0) * (1.0 / total)
    work = jnp.concatenate([gram, (row == col).astype(jnp.float32)], axis=1)
    bands = [work[8 * at : 8 * at + 8] for at in range(K // 8)]
    place = lax.broadcasted_iota(jnp.int32, (8, 1), 0)
    for at in range(K):
        band, inside = divmod(at, 8)
        pivot_row = bands[band][inside : inside + 1, :]
        inverse = 1.0 / pivot_row[:, at : at + 1]
        for under in range(band, K // 8):
            factor = bands[under][:, at : at + 1] * inverse
            if under == band:
                factor = jnp.where(place > inside, factor, 0.0)
            bands[under] = bands[under] - factor * pivot_row
    work = jnp.concatenate(bands, axis=0)
    pivots = jnp.sum(jnp.where(row == col, work[:, :K], 0.0), axis=1, keepdims=True)
    out_ref[...] = work[:, K:] * lax.rsqrt(pivots)


def turn_kernel(tile_ref, *refs):
    out_ref = refs[-1]
    for at in range(tile_ref.shape[0]):
        out_ref[at] = tile_ref[at].T


def turned_tiles(tiles, first, blocks, into):
    size = tiles.shape[0] // 16
    block = pl.BlockSpec((size, TILE, TILE), lambda step: (step + first, 0, 0))
    return pl.pallas_call(
        turn_kernel,
        out_shape=jax.ShapeDtypeStruct(tiles.shape, tiles.dtype),
        grid=(blocks,),
        in_specs=[block] + ([] if into is None else [pl.BlockSpec(memory_space=pl.ANY)]),
        out_specs=block,
        input_output_aliases={} if into is None else {1: 0},
        name="turned_tiles",
    )(*([tiles] if into is None else [tiles, into]))


def inverse_factor(gram, total):
    return pl.pallas_call(
        functools.partial(factor_kernel, total=total),
        out_shape=jax.ShapeDtypeStruct((K, K), jnp.float32),
        in_specs=[VMEM_SPEC],
        out_specs=VMEM_SPEC,
        name="factor",
    )(gram)


def scale_kernel(*refs, factored):
    refs = list(refs)
    inverse = refs.pop(0)[...] if factored else None
    raw_refs, refs = list(zip(refs[:PARTS], refs[PARTS : 2 * PARTS])), refs[2 * PARTS :]
    scale_ref, panel_ref, sent_refs = refs[0], refs[1], refs[2:]
    blocks = scale_ref.shape[0]
    gram = jnp.zeros((K, K), jnp.float32)
    for at in range(blocks):
        scale = scale_ref[at][None, :]
        panel = jnp.concatenate([kept[at] + got[at] for kept, got in raw_refs], axis=0)
        if factored:
            panel = dot_full(inverse, panel, (1, 0))
        panel = scale * panel
        panel_ref[at] = panel
        for part in range(PARTS):
            sent_refs[part][at] = scale * panel[part * ROWS : (part + 1) * ROWS]
        gram = gram + dot_full(panel, panel, (1, 1))
    sent_refs[0][blocks] = jnp.concatenate([gram[:ROWS], gram[ROWS:]], axis=1)


def scale_panel(inverse, kept, got, scale):
    factored = inverse is not None
    operands = ([inverse] if factored else []) + list(kept) + list(got) + [scale]
    blocks = scale.shape[0]
    panel, *sent = pl.pallas_call(
        functools.partial(scale_kernel, factored=factored),
        out_shape=[jax.ShapeDtypeStruct((blocks, K, TILE), jnp.float32)]
        + [jax.ShapeDtypeStruct((blocks + (part == 0), ROWS, TILE), jnp.float32) for part in range(PARTS)],
        in_specs=[VMEM_SPEC] * len(operands),
        out_specs=[VMEM_SPEC] * (1 + PARTS),
        name="scale_panel",
    )(*operands)
    return panel, sent


def finish_kernel(inverse_ref, panel_ref, out_ref):
    for at in range(panel_ref.shape[0]):
        out_ref[:, at * TILE : (at + 1) * TILE] = dot_full(inverse_ref[...], panel_ref[at], (1, 0))


def finish_panel(inverse, panel):
    return pl.pallas_call(
        finish_kernel,
        out_shape=jax.ShapeDtypeStruct((K, panel.shape[0] * TILE), jnp.float32),
        in_specs=[VMEM_SPEC] * 2,
        out_specs=VMEM_SPEC,
        name="finish_panel",
    )(inverse, panel)


def body(tile_rows, tile_cols, tile_count, tile_vals, user_degree, item_degree, start_items):
    user_groups = lax.axis_size("users")
    item_groups = lax.axis_size("items")
    user_blocks = UT // item_groups
    item_blocks = IT // user_groups
    user_total = UT * TILE * user_groups
    item_total = IT * TILE * item_groups

    rows = tile_rows[0, 0]
    cols = tile_cols[0, 0]
    tiles = tile_vals[0, 0]
    count = tile_count[0]
    live = jnp.arange(rows.shape[0], dtype=jnp.int32) < count[0]
    row_at = relative_position(rows // user_blocks, "items", 0) * user_blocks + rows % user_blocks
    col_at = relative_position(cols // item_blocks, "users", 0) * item_blocks + cols % item_blocks
    row_to = jnp.where(live, row_at, UT)
    col_to = jnp.where(live, col_at, IT)

    user_scale = lax.rsqrt(user_degree.astype(jnp.float32)).reshape(user_blocks, TILE)
    item_scale = lax.rsqrt(item_degree.astype(jnp.float32)).reshape(item_blocks, TILE)
    start = start_items.astype(jnp.float32).reshape(PARTS, ROWS, item_blocks, TILE).transpose(0, 2, 1, 3)
    start = item_scale[None, :, None, :] * start
    sent = [jnp.concatenate([start[0], jnp.zeros_like(start[0][:1])], axis=0), start[1]]
    turned = turned_tiles(tiles, 0, 8, None)
    turned = turned_tiles(tiles, 8, 8, turned)
    item_inverse = None
    for step in range(ITERS):
        pieces = gather(sent, "users")
        kept, out = tiles_product(count, col_at, row_to, pieces, turned, UT, "users", "items")
        kept, got, gram = reduce_scatter(kept, out, "items")
        if step:
            item_inverse = inverse_factor(gram, item_total)
        user_raw, sent = scale_panel(item_inverse, kept, got, user_scale)
        pieces = gather(sent, "items")
        kept, out = tiles_product(count, row_at, col_to, pieces, tiles, IT, "items", "users")
        kept, got, gram = reduce_scatter(kept, out, "users")
        user_inverse = inverse_factor(gram, user_total)
        if step == ITERS - 1:
            user_panel = finish_panel(user_inverse, user_raw)
            user_panel, got = lax.optimization_barrier((user_panel, got))
        item_raw, sent = scale_panel(user_inverse, kept, got, item_scale)
    item_inverse = inverse_factor(all_sum(sent[0][-1]), item_total)
    return user_panel, finish_panel(item_inverse, item_raw)


def solution(mesh):
    in_specs = (
        P("users", "items", None),
        P("users", "items", None),
        P("users", "items"),
        P("users", "items", None, None, None),
        P(("users", "items")),
        P(("items", "users")),
        P(None, ("items", "users")),
    )
    out_specs = (P(None, ("users", "items")), P(None, ("items", "users")))
    return jax.shard_map(body, mesh=mesh, in_specs=in_specs, out_specs=out_specs, check_vma=False)
```

```python
import functools

import jax
import jax.numpy as jnp
from jax import lax
from jax.experimental import pallas as pl
from jax.experimental.pallas import tpu as pltpu
from jax.sharding import PartitionSpec as P


K = 64
PARTS = 4
ROWS = K // PARTS
TILE = 128
GRAM = K // 2 // ROWS
ITERS = 2
UT = 64
IT = 64
BATCH = 64
UNROLL = 64
HIGHEST = lax.Precision.HIGHEST
VMEM_SPEC = pl.BlockSpec(memory_space=pltpu.VMEM)


def gather_order(axis, part):
    order = []
    bit = lax.axis_size(axis) >> 1
    while bit:
        order.append(bit)
        bit >>= 1
    if axis == "users" and part % 2 == 1:
        order[-2:] = order[-2:][::-1]
    return order


def exchange(value, axis, bit):
    return lax.ppermute(value, axis, [(at, at ^ bit) for at in range(lax.axis_size(axis))])


def relative_position(shard, axis, part):
    apart = shard ^ lax.axis_index(axis)
    place = jnp.zeros_like(apart)
    for level, bit in enumerate(gather_order(axis, part)):
        place = place + jnp.where(apart & bit != 0, 1 << level, 0)
    return place


def gather(held, axis):
    held = list(held)
    levels = len(gather_order(axis, 0))
    for level in range(levels - 2):
        got = []
        for part in range(PARTS):
            got.append(exchange(held[part], axis, gather_order(axis, part)[level]))
        first = jnp.concatenate([held[0][:-GRAM], got[0][:-GRAM], held[0][-GRAM:] + got[0][-GRAM:]], axis=0)
        held = [first] + [jnp.concatenate([have, more], axis=0) for have, more in zip(held[1:], got[1:])]
    order = [gather_order(axis, part)[-2:] for part in range(PARTS)]
    near, own, far = [], [], []
    for part in range(PARTS):
        near.append(exchange(held[part], axis, order[part][0]))
        own.append(exchange(held[part], axis, order[part][1]))
    for part in range(PARTS):
        far.append(exchange(near[part], axis, order[part][1]))
    return [[held[part], near[part], own[part], far[part]] for part in range(PARTS)]


def reduce_scatter(kept, sent, gram, axis):
    for level in range(len(gather_order(axis, 0)) - 1, -1, -1):
        other = exchange(gram, axis, gather_order(axis, 0)[level])
        got = []
        for part in range(PARTS):
            got.append(exchange(sent[part], axis, gather_order(axis, part)[level]))
        gram = gram + other
        if level:
            half = kept[0].shape[0] // 2
            sent = [have[half:] + more[half:] for have, more in zip(kept, got)]
            kept = [have[:half] + more[:half] for have, more in zip(kept, got)]
    return kept, got, gram


def all_sum(value):
    for axis in ("items", "users"):
        for bit in gather_order(axis, 0)[::-1]:
            value = value + exchange(value, axis, bit)
    return value


def part_places(axis, part, blocks):
    swapped = gather_order(axis, part) != gather_order(axis, 0)
    quarter = blocks // 4
    return [at * quarter for at in ((0, 2, 1, 3) if swapped else (0, 1, 2, 3))], quarter


def tiles_kernel(count, source, target, *refs, places_in, places_out):
    piece_refs, refs = [refs[4 * part : 4 * part + 4] for part in range(PARTS)], refs[4 * PARTS :]
    tile_ref, keep_refs, send_refs = refs[0], refs[1 : 1 + PARTS], refs[1 + PARTS : 1 + 2 * PARTS]
    gram_ref, pieces, total = refs[1 + 2 * PARTS :]
    step = pl.program_id(0)
    half_out = keep_refs[-1].shape[0]

    @pl.when(step == 0)
    def _():
        for part in range(PARTS):
            starts, quarter = places_in[part]
            band = slice(part * ROWS, (part + 1) * ROWS)
            for at, place in enumerate(starts):
                ref = piece_refs[part][at]

                def prepare(block, carry):
                    value = ref[block]
                    top = value.astype(jnp.bfloat16)
                    pieces[place + block, band, :TILE] = top
                    pieces[place + block, band, TILE:] = (value - top.astype(jnp.float32)).astype(jnp.bfloat16)
                    return carry

                lax.fori_loop(0, quarter, prepare, 0, unroll=4)

        def clear(at, carry):
            total[at] = jnp.zeros((K, TILE), jnp.float32)
            return carry

        lax.fori_loop(0, 2 * half_out, clear, 0, unroll=4)

    live = jnp.clip(count[0] - step * BATCH, 0, BATCH)

    def group(at, carry):
        first = at * UNROLL
        products = []
        for slot in range(UNROLL):
            tile = tile_ref[first + slot]
            products.append(
                lax.dot_general(
                    pieces[source[step * BATCH + first + slot]],
                    jnp.concatenate([tile, tile], axis=0),
                    (((1,), (0,)), ((), ())),
                    preferred_element_type=jnp.float32,
                )
            )
        for slot in range(UNROLL):
            total[target[step * BATCH + first + slot]] += products[slot]
        return carry

    lax.fori_loop(0, (live + UNROLL - 1) // UNROLL, group, 0)

    @pl.when(step == pl.num_programs(0) - 1)
    def _():
        for part in range(PARTS):
            starts, quarter = places_out[part]
            band = slice(part * ROWS, (part + 1) * ROWS)
            for at, place in enumerate(starts):
                ref = (keep_refs, keep_refs, send_refs, send_refs)[at][part]
                first = at % 2 * quarter

                def finish(block, carry):
                    ref[first + block] = total[place + block, band]
                    return carry

                lax.fori_loop(0, quarter, finish, 0, unroll=4)
        for at in range(GRAM):
            held, near, own, far = [ref[ref.shape[0] - GRAM + at] for ref in piece_refs[0]]
            gram_ref[at * ROWS : (at + 1) * ROWS] = (held + near) + (own + far)


def tiles_product(count, source, target, pieces, tiles, blocks_out, axis_in, axis_out):
    quarter_in = pieces[-1][0].shape[0]
    half_out = blocks_out // 2

    def tile_block(step, count, source, target):
        return (jnp.minimum(step, (count[0] + BATCH - 1) // BATCH - 1), 0, 0)

    kernel = functools.partial(
        tiles_kernel,
        places_in=[part_places(axis_in, part, 4 * quarter_in) for part in range(PARTS)],
        places_out=[part_places(axis_out, part, 2 * half_out) for part in range(PARTS)],
    )
    out = pl.pallas_call(
        kernel,
        out_shape=[jax.ShapeDtypeStruct((half_out, ROWS, TILE), jnp.float32)] * (2 * PARTS)
        + [jax.ShapeDtypeStruct((K // 2, TILE), jnp.float32)],
        grid_spec=pltpu.PrefetchScalarGridSpec(
            num_scalar_prefetch=3,
            grid=(tiles.shape[0] // BATCH,),
            in_specs=[VMEM_SPEC] * (4 * PARTS)
            + [pl.BlockSpec((BATCH, TILE, TILE), tile_block)],
            out_specs=[VMEM_SPEC] * (2 * PARTS + 1),
            scratch_shapes=[
                pltpu.VMEM((4 * quarter_in, K, 2 * TILE), jnp.bfloat16),
                pltpu.VMEM((2 * half_out + 1, K, TILE), jnp.float32),
            ],
        ),
    )(count, source, target, *[piece for part in pieces for piece in part], tiles)
    return out[:PARTS], out[PARTS : 2 * PARTS], out[-1]


def dot_full(left, right, contract):
    return lax.dot_general(
        left, right, ((contract[:1], contract[1:]), ((), ())), precision=HIGHEST, preferred_element_type=jnp.float32
    )


def factor_kernel(gram_ref, out_ref, *, total):
    row = lax.broadcasted_iota(jnp.int32, (K, K), 0)
    col = lax.broadcasted_iota(jnp.int32, (K, K), 1)
    gram = jnp.concatenate([gram_ref[:, :K], gram_ref[:, K:]], axis=0) * (1.0 / total)
    work = jnp.concatenate([gram, (row == col).astype(jnp.float32)], axis=1)
    bands = [work[8 * at : 8 * at + 8] for at in range(K // 8)]
    place = lax.broadcasted_iota(jnp.int32, (8, 1), 0)
    for at in range(K):
        band, inside = divmod(at, 8)
        pivot_row = bands[band][inside : inside + 1, :]
        inverse = 1.0 / pivot_row[:, at : at + 1]
        for under in range(band, K // 8):
            factor = bands[under][:, at : at + 1] * inverse
            if under == band:
                factor = jnp.where(place > inside, factor, 0.0)
            bands[under] = bands[under] - factor * pivot_row
    work = jnp.concatenate(bands, axis=0)
    pivots = jnp.sum(jnp.where(row == col, work[:, :K], 0.0), axis=1, keepdims=True)
    out_ref[...] = work[:, K:] * lax.rsqrt(pivots)


def turn_kernel(tile_ref, *refs):
    out_ref = refs[-1]
    for at in range(tile_ref.shape[0]):
        out_ref[at] = tile_ref[at].T


def turned_tiles(tiles, first, blocks, into):
    size = tiles.shape[0] // 16
    block = pl.BlockSpec((size, TILE, TILE), lambda step: (step + first, 0, 0))
    return pl.pallas_call(
        turn_kernel,
        out_shape=jax.ShapeDtypeStruct(tiles.shape, tiles.dtype),
        grid=(blocks,),
        in_specs=[block] + ([] if into is None else [pl.BlockSpec(memory_space=pl.ANY)]),
        out_specs=block,
        input_output_aliases={} if into is None else {1: 0},
        name="turned_tiles",
    )(*([tiles] if into is None else [tiles, into]))


def inverse_factor(gram, total):
    return pl.pallas_call(
        functools.partial(factor_kernel, total=total),
        out_shape=jax.ShapeDtypeStruct((K, K), jnp.float32),
        in_specs=[VMEM_SPEC],
        out_specs=VMEM_SPEC,
        name="factor",
    )(gram)


def scale_kernel(*refs, factored):
    refs = list(refs)
    inverse = refs.pop(0)[...] if factored else None
    raw_refs, refs = list(zip(refs[:PARTS], refs[PARTS : 2 * PARTS])), refs[2 * PARTS :]
    scale_ref, panel_ref, sent_refs = refs[0], refs[1], refs[2:]
    blocks = scale_ref.shape[0]
    gram = jnp.zeros((K, K), jnp.float32)
    for at in range(blocks):
        scale = scale_ref[at][None, :]
        panel = jnp.concatenate([kept[at] + got[at] for kept, got in raw_refs], axis=0)
        if factored:
            panel = dot_full(inverse, panel, (1, 0))
        panel = scale * panel
        panel_ref[at] = panel
        for part in range(PARTS):
            sent_refs[part][at] = scale * panel[part * ROWS : (part + 1) * ROWS]
        gram = gram + dot_full(panel, panel, (1, 1))
    gram = jnp.concatenate([gram[: K // 2], gram[K // 2 :]], axis=1)
    for at in range(GRAM):
        sent_refs[0][blocks + at] = gram[at * ROWS : (at + 1) * ROWS]


def scale_panel(inverse, kept, got, scale):
    factored = inverse is not None
    operands = ([inverse] if factored else []) + list(kept) + list(got) + [scale]
    blocks = scale.shape[0]
    panel, *sent = pl.pallas_call(
        functools.partial(scale_kernel, factored=factored),
        out_shape=[jax.ShapeDtypeStruct((blocks, K, TILE), jnp.float32)]
        + [jax.ShapeDtypeStruct((blocks + GRAM * (part == 0), ROWS, TILE), jnp.float32) for part in range(PARTS)],
        in_specs=[VMEM_SPEC] * len(operands),
        out_specs=[VMEM_SPEC] * (1 + PARTS),
        name="scale_panel",
    )(*operands)
    return panel, sent


def finish_kernel(inverse_ref, panel_ref, out_ref):
    for at in range(panel_ref.shape[0]):
        out_ref[:, at * TILE : (at + 1) * TILE] = dot_full(inverse_ref[...], panel_ref[at], (1, 0))


def finish_panel(inverse, panel):
    return pl.pallas_call(
        finish_kernel,
        out_shape=jax.ShapeDtypeStruct((K, panel.shape[0] * TILE), jnp.float32),
        in_specs=[VMEM_SPEC] * 2,
        out_specs=VMEM_SPEC,
        name="finish_panel",
    )(inverse, panel)


def body(tile_rows, tile_cols, tile_count, tile_vals, user_degree, item_degree, start_items):
    user_groups = lax.axis_size("users")
    item_groups = lax.axis_size("items")
    user_blocks = UT // item_groups
    item_blocks = IT // user_groups
    user_total = UT * TILE * user_groups
    item_total = IT * TILE * item_groups

    rows = tile_rows[0, 0]
    cols = tile_cols[0, 0]
    tiles = tile_vals[0, 0]
    count = tile_count[0]
    live = jnp.arange(rows.shape[0], dtype=jnp.int32) < count[0]
    row_at = relative_position(rows // user_blocks, "items", 0) * user_blocks + rows % user_blocks
    col_at = relative_position(cols // item_blocks, "users", 0) * item_blocks + cols % item_blocks
    row_to = jnp.where(live, row_at, UT)
    col_to = jnp.where(live, col_at, IT)

    user_scale = lax.rsqrt(user_degree.astype(jnp.float32)).reshape(user_blocks, TILE)
    item_scale = lax.rsqrt(item_degree.astype(jnp.float32)).reshape(item_blocks, TILE)
    start = start_items.astype(jnp.float32).reshape(PARTS, ROWS, item_blocks, TILE).transpose(0, 2, 1, 3)
    start = item_scale[None, :, None, :] * start
    sent = [start[part] for part in range(PARTS)]
    sent[0] = jnp.concatenate([sent[0], jnp.zeros((GRAM, ROWS, TILE), jnp.float32)], axis=0)
    turned = turned_tiles(tiles, 0, 8, None)
    turned = turned_tiles(tiles, 8, 8, turned)
    item_inverse = None
    for step in range(ITERS):
        pieces = gather(sent, "users")
        kept, out, gram = tiles_product(count, col_at, row_to, pieces, turned, UT, "users", "items")
        kept, got, gram = reduce_scatter(kept, out, gram, "items")
        if step:
            item_inverse = inverse_factor(gram, item_total)
        user_raw, sent = scale_panel(item_inverse, kept, got, user_scale)
        pieces = gather(sent, "items")
        kept, out, gram = tiles_product(count, row_at, col_to, pieces, tiles, IT, "items", "users")
        kept, got, gram = reduce_scatter(kept, out, gram, "users")
        user_inverse = inverse_factor(gram, user_total)
        if step == ITERS - 1:
            user_panel = finish_panel(user_inverse, user_raw)
            user_panel, got = lax.optimization_barrier((user_panel, got))
        item_raw, sent = scale_panel(user_inverse, kept, got, item_scale)
    item_inverse = inverse_factor(all_sum(sent[0][-GRAM:].reshape(K // 2, TILE)), item_total)
    return user_panel, finish_panel(item_inverse, item_raw)


def solution(mesh):
    in_specs = (
        P("users", "items", None),
        P("users", "items", None),
        P("users", "items"),
        P("users", "items", None, None, None),
        P(("users", "items")),
        P(("items", "users")),
        P(None, ("items", "users")),
    )
    out_specs = (P(None, ("users", "items")), P(None, ("items", "users")))
    return jax.shard_map(body, mesh=mesh, in_specs=in_specs, out_specs=out_specs, check_vma=False)
```

```python
import functools

import jax
import jax.numpy as jnp
from jax import lax
from jax.experimental import pallas as pl
from jax.experimental.pallas import tpu as pltpu
from jax.sharding import PartitionSpec as P


K = 64
PARTS = 2
ROWS = K // PARTS
TILE = 128
ITERS = 2
UT = 64
IT = 64
BATCH = 64
UNROLL = 64
HIGHEST = lax.Precision.HIGHEST
VMEM_SPEC = pl.BlockSpec(memory_space=pltpu.VMEM)


def gather_order(axis, part):
    order = []
    bit = lax.axis_size(axis) >> 1
    while bit:
        order.append(bit)
        bit >>= 1
    if axis == "users" and part % 2 == 1:
        order[-2:] = order[-2:][::-1]
    return order


def exchange(value, axis, bit):
    return lax.ppermute(value, axis, [(at, at ^ bit) for at in range(lax.axis_size(axis))])


def relative_position(shard, axis, part):
    apart = shard ^ lax.axis_index(axis)
    place = jnp.zeros_like(apart)
    for level, bit in enumerate(gather_order(axis, part)):
        place = place + jnp.where(apart & bit != 0, 1 << level, 0)
    return place


def gather(held, axis):
    held = list(held)
    levels = len(gather_order(axis, 0))
    for level in range(levels - 2):
        got = []
        for part in range(PARTS):
            got.append(exchange(held[part], axis, gather_order(axis, part)[level]))
        held = [jnp.concatenate([have, more], axis=0) for have, more in zip(held, got)]
    order = [gather_order(axis, part)[-2:] for part in range(PARTS)]
    near, own, far = [], [], []
    for part in range(PARTS):
        near.append(exchange(held[part], axis, order[part][0]))
        own.append(exchange(held[part], axis, order[part][1]))
    for part in range(PARTS):
        far.append(exchange(near[part], axis, order[part][1]))
    return [[held[part], near[part], own[part], far[part]] for part in range(PARTS)]


def reduce_scatter(kept, sent, axis):
    for level in range(len(gather_order(axis, 0)) - 1, -1, -1):
        got = []
        for part in range(PARTS):
            got.append(exchange(sent[part], axis, gather_order(axis, part)[level]))
        if level:
            half = kept[0].shape[0] // 2
            sent = [have[half:] + more[half:] for have, more in zip(kept, got)]
            kept = [have[:half] + more[:half] for have, more in zip(kept, got)]
    return kept, got


def sum_over(value, axis):
    for bit in gather_order(axis, 0)[::-1]:
        other = exchange(value, axis, bit)
        value = value + other
    return value


def part_places(axis, part, blocks):
    swapped = gather_order(axis, part) != gather_order(axis, 0)
    quarter = blocks // 4
    return [at * quarter for at in ((0, 2, 1, 3) if swapped else (0, 1, 2, 3))], quarter


def tiles_kernel(count, source, target, *refs, places_in, places_out):
    piece_refs, refs = [refs[4 * part : 4 * part + 4] for part in range(PARTS)], refs[4 * PARTS :]
    tile_ref, keep_refs, send_refs = refs[0], refs[1 : 1 + PARTS], refs[1 + PARTS : 1 + 2 * PARTS]
    pieces, total = refs[1 + 2 * PARTS :]
    step = pl.program_id(0)
    half_out = keep_refs[-1].shape[0]

    @pl.when(step == 0)
    def _():
        for part in range(PARTS):
            starts, quarter = places_in[part]
            band = slice(part * ROWS, (part + 1) * ROWS)
            for at, place in enumerate(starts):
                ref = piece_refs[part][at]

                def prepare(block, carry):
                    value = ref[block]
                    top = value.astype(jnp.bfloat16)
                    pieces[place + block, band, :TILE] = top
                    pieces[place + block, band, TILE:] = (value - top.astype(jnp.float32)).astype(jnp.bfloat16)
                    return carry

                lax.fori_loop(0, quarter, prepare, 0, unroll=4)

        def clear(at, carry):
            total[at] = jnp.zeros((K, TILE), jnp.float32)
            return carry

        lax.fori_loop(0, 2 * half_out, clear, 0, unroll=4)

    live = jnp.clip(count[0] - step * BATCH, 0, BATCH)

    def group(at, carry):
        first = at * UNROLL
        products = []
        for slot in range(UNROLL):
            tile = tile_ref[first + slot]
            products.append(
                lax.dot_general(
                    pieces[source[step * BATCH + first + slot]],
                    jnp.concatenate([tile, tile], axis=0),
                    (((1,), (0,)), ((), ())),
                    preferred_element_type=jnp.float32,
                )
            )
        for slot in range(UNROLL):
            total[target[step * BATCH + first + slot]] += products[slot]
        return carry

    lax.fori_loop(0, (live + UNROLL - 1) // UNROLL, group, 0)

    @pl.when(step == pl.num_programs(0) - 1)
    def _():
        for part in range(PARTS):
            starts, quarter = places_out[part]
            band = slice(part * ROWS, (part + 1) * ROWS)
            for at, place in enumerate(starts):
                ref = (keep_refs, keep_refs, send_refs, send_refs)[at][part]
                first = at % 2 * quarter

                def finish(block, carry):
                    ref[first + block] = total[place + block, band]
                    return carry

                lax.fori_loop(0, quarter, finish, 0, unroll=4)


def tiles_product(count, source, target, pieces, tiles, blocks_out, axis_in, axis_out):
    quarter_in = pieces[-1][0].shape[0]
    half_out = blocks_out // 2

    def tile_block(step, count, source, target):
        return (jnp.minimum(step, (count[0] + BATCH - 1) // BATCH - 1), 0, 0)

    kernel = functools.partial(
        tiles_kernel,
        places_in=[part_places(axis_in, part, 4 * quarter_in) for part in range(PARTS)],
        places_out=[part_places(axis_out, part, 2 * half_out) for part in range(PARTS)],
    )
    call = pl.pallas_call(
        kernel,
        out_shape=[jax.ShapeDtypeStruct((half_out, ROWS, TILE), jnp.float32)] * (2 * PARTS),
        grid_spec=pltpu.PrefetchScalarGridSpec(
            num_scalar_prefetch=3,
            grid=(tiles.shape[0] // BATCH,),
            in_specs=[VMEM_SPEC] * (4 * PARTS)
            + [pl.BlockSpec((BATCH, TILE, TILE), tile_block)],
            out_specs=[VMEM_SPEC] * (2 * PARTS),
            scratch_shapes=[
                pltpu.VMEM((4 * quarter_in, K, 2 * TILE), jnp.bfloat16),
                pltpu.VMEM((2 * half_out + 1, K, TILE), jnp.float32),
            ],
        ),
    )
    out = call(count, source, target, *[piece for part in pieces for piece in part], tiles)
    return out[:PARTS], out[PARTS:]


def dot_full(left, right, contract):
    return lax.dot_general(
        left, right, ((contract[:1], contract[1:]), ((), ())), precision=HIGHEST, preferred_element_type=jnp.float32
    )


def factor_kernel(gram_ref, out_ref, *, total):
    row = lax.broadcasted_iota(jnp.int32, (K, K), 0)
    col = lax.broadcasted_iota(jnp.int32, (K, K), 1)
    gram = jnp.concatenate([gram_ref[:, :K], gram_ref[:, K:]], axis=0) * (1.0 / total)
    work = jnp.concatenate([gram, (row == col).astype(jnp.float32)], axis=1)
    bands = [work[8 * at : 8 * at + 8] for at in range(K // 8)]
    place = lax.broadcasted_iota(jnp.int32, (8, 1), 0)
    for at in range(K):
        band, inside = divmod(at, 8)
        pivot_row = bands[band][inside : inside + 1, :]
        inverse = 1.0 / pivot_row[:, at : at + 1]
        for under in range(band, K // 8):
            factor = bands[under][:, at : at + 1] * inverse
            if under == band:
                factor = jnp.where(place > inside, factor, 0.0)
            bands[under] = bands[under] - factor * pivot_row
    work = jnp.concatenate(bands, axis=0)
    pivots = jnp.sum(jnp.where(row == col, work[:, :K], 0.0), axis=1, keepdims=True)
    out_ref[...] = work[:, K:] * lax.rsqrt(pivots)


def turn_kernel(tile_ref, *refs):
    out_ref = refs[-1]
    for at in range(tile_ref.shape[0]):
        out_ref[at] = tile_ref[at].T


def turned_tiles(tiles, first, blocks, into):
    size = tiles.shape[0] // 16
    block = pl.BlockSpec((size, TILE, TILE), lambda step: (step + first, 0, 0))
    return pl.pallas_call(
        turn_kernel,
        out_shape=jax.ShapeDtypeStruct(tiles.shape, tiles.dtype),
        grid=(blocks,),
        in_specs=[block] + ([] if into is None else [pl.BlockSpec(memory_space=pl.ANY)]),
        out_specs=block,
        input_output_aliases={} if into is None else {1: 0},
        name="turned_tiles",
    )(*([tiles] if into is None else [tiles, into]))


def inverse_factor(gram, total):
    return pl.pallas_call(
        functools.partial(factor_kernel, total=total),
        out_shape=jax.ShapeDtypeStruct((K, K), jnp.float32),
        in_specs=[VMEM_SPEC],
        out_specs=VMEM_SPEC,
        name="factor",
    )(gram)


def scale_kernel(*refs, factored):
    refs = list(refs)
    inverse = refs.pop(0)[...] if factored else None
    raw_refs, refs = list(zip(refs[:PARTS], refs[PARTS : 2 * PARTS])), refs[2 * PARTS :]
    scale_ref, panel_ref, gram_ref, sent_refs = refs[0], refs[1], refs[2], refs[3:]
    blocks = scale_ref.shape[0]
    gram = jnp.zeros((K, K), jnp.float32)
    for at in range(blocks):
        scale = scale_ref[at][None, :]
        panel = jnp.concatenate([kept[at] + got[at] for kept, got in raw_refs], axis=0)
        if factored:
            panel = dot_full(inverse, panel, (1, 0))
        panel = scale * panel
        panel_ref[at] = panel
        for part in range(PARTS):
            sent_refs[part][at] = scale * panel[part * ROWS : (part + 1) * ROWS]
        gram = gram + dot_full(panel, panel, (1, 1))
    gram_ref[...] = jnp.concatenate([gram[: K // 2], gram[K // 2 :]], axis=1)


def scale_panel(inverse, kept, got, scale):
    factored = inverse is not None
    operands = ([inverse] if factored else []) + list(kept) + list(got) + [scale]
    blocks = scale.shape[0]
    panel, gram, *sent = pl.pallas_call(
        functools.partial(scale_kernel, factored=factored),
        out_shape=[jax.ShapeDtypeStruct((blocks, K, TILE), jnp.float32)]
        + [jax.ShapeDtypeStruct((K // 2, TILE), jnp.float32)]
        + [jax.ShapeDtypeStruct((blocks, ROWS, TILE), jnp.float32)] * PARTS,
        in_specs=[VMEM_SPEC] * len(operands),
        out_specs=[VMEM_SPEC] * (2 + PARTS),
        name="scale_panel",
    )(*operands)
    return panel, sent, gram


def finish_kernel(inverse_ref, panel_ref, out_ref):
    for at in range(panel_ref.shape[0]):
        out_ref[:, at * TILE : (at + 1) * TILE] = dot_full(inverse_ref[...], panel_ref[at], (1, 0))


def finish_panel(inverse, panel):
    return pl.pallas_call(
        finish_kernel,
        out_shape=jax.ShapeDtypeStruct((K, panel.shape[0] * TILE), jnp.float32),
        in_specs=[VMEM_SPEC] * 2,
        out_specs=VMEM_SPEC,
        name="finish_panel",
    )(inverse, panel)


def body(tile_rows, tile_cols, tile_count, tile_vals, user_degree, item_degree, start_items):
    user_groups = lax.axis_size("users")
    item_groups = lax.axis_size("items")
    user_blocks = UT // item_groups
    item_blocks = IT // user_groups
    user_total = UT * TILE * user_groups
    item_total = IT * TILE * item_groups

    rows = tile_rows[0, 0]
    cols = tile_cols[0, 0]
    tiles = tile_vals[0, 0]
    count = tile_count[0]
    live = jnp.arange(rows.shape[0], dtype=jnp.int32) < count[0]
    row_at = relative_position(rows // user_blocks, "items", 0) * user_blocks + rows % user_blocks
    col_at = relative_position(cols // item_blocks, "users", 0) * item_blocks + cols % item_blocks
    row_to = jnp.where(live, row_at, UT)
    col_to = jnp.where(live, col_at, IT)

    user_scale = lax.rsqrt(user_degree.astype(jnp.float32)).reshape(user_blocks, TILE)
    item_scale = lax.rsqrt(item_degree.astype(jnp.float32)).reshape(item_blocks, TILE)
    start = start_items.astype(jnp.float32).reshape(PARTS, ROWS, item_blocks, TILE).transpose(0, 2, 1, 3)
    start = item_scale[None, :, None, :] * start
    sent = [start[part] for part in range(PARTS)]
    turned = turned_tiles(tiles, 0, 8, None)
    turned = turned_tiles(tiles, 8, 8, turned)
    item_inverse = item_gram = None
    for step in range(ITERS):
        if step:
            item_gram = sum_over(sum_over(item_gram, "items"), "users")
            item_inverse = inverse_factor(item_gram, item_total)
        pieces = gather(sent, "users")
        kept, out = tiles_product(count, col_at, row_to, pieces, turned, UT, "users", "items")
        kept, got = reduce_scatter(kept, out, "items")
        user_raw, sent, user_gram = scale_panel(item_inverse, kept, got, user_scale)
        user_gram = sum_over(sum_over(user_gram, "users"), "items")
        user_inverse = inverse_factor(user_gram, user_total)
        pieces = gather(sent, "items")
        kept, out = tiles_product(count, row_at, col_to, pieces, tiles, IT, "items", "users")
        kept, got = reduce_scatter(kept, out, "users")
        if step == ITERS - 1:
            user_panel = finish_panel(user_inverse, user_raw)
            user_panel, got = lax.optimization_barrier((user_panel, got))
        item_raw, sent, item_gram = scale_panel(user_inverse, kept, got, item_scale)
    item_gram = sum_over(sum_over(item_gram, "items"), "users")
    return user_panel, finish_panel(inverse_factor(item_gram, item_total), item_raw)


def solution(mesh):
    in_specs = (
        P("users", "items", None),
        P("users", "items", None),
        P("users", "items"),
        P("users", "items", None, None, None),
        P(("users", "items")),
        P(("items", "users")),
        P(None, ("items", "users")),
    )
    out_specs = (P(None, ("users", "items")), P(None, ("items", "users")))
    return jax.shard_map(body, mesh=mesh, in_specs=in_specs, out_specs=out_specs, check_vma=False)
```

```python
import functools

import jax
import jax.numpy as jnp
from jax import lax
from jax.experimental import pallas as pl
from jax.experimental.pallas import tpu as pltpu
from jax.sharding import PartitionSpec as P


K = 64
PARTS = 4
ROWS = K // PARTS
TILE = 128
GRAM = K // 2 // ROWS
ITERS = 2
UT = 64
IT = 64
BATCH = 64
UNROLL = 64
HIGHEST = lax.Precision.HIGHEST
VMEM_SPEC = pl.BlockSpec(memory_space=pltpu.VMEM)


def gather_order(axis, part):
    order = []
    bit = lax.axis_size(axis) >> 1
    while bit:
        order.append(bit)
        bit >>= 1
    if axis == "users" and part % 2 == 1:
        order[-2:] = order[-2:][::-1]
    return order


def exchange(value, axis, bit):
    return lax.ppermute(value, axis, [(at, at ^ bit) for at in range(lax.axis_size(axis))])


def relative_position(shard, axis, part):
    apart = shard ^ lax.axis_index(axis)
    place = jnp.zeros_like(apart)
    for level, bit in enumerate(gather_order(axis, part)):
        place = place + jnp.where(apart & bit != 0, 1 << level, 0)
    return place


def gather(held, axis):
    held = list(held)
    levels = len(gather_order(axis, 0))
    for level in range(levels - 2):
        got = []
        for part in range(PARTS):
            got.append(exchange(held[part], axis, gather_order(axis, part)[level]))
        first = jnp.concatenate([held[0][:-GRAM], got[0][:-GRAM], held[0][-GRAM:] + got[0][-GRAM:]], axis=0)
        held = [first] + [jnp.concatenate([have, more], axis=0) for have, more in zip(held[1:], got[1:])]
    order = [gather_order(axis, part)[-2:] for part in range(PARTS)]
    near, own, far = [], [], []
    for part in range(PARTS):
        near.append(exchange(held[part], axis, order[part][0]))
        own.append(exchange(held[part], axis, order[part][1]))
    for part in range(PARTS):
        far.append(exchange(near[part], axis, order[part][1]))
    return [[held[part], near[part], own[part], far[part]] for part in range(PARTS)]


def reduce_scatter(kept, sent, axis):
    for level in range(len(gather_order(axis, 0)) - 1, -1, -1):
        got = []
        for part in range(PARTS):
            got.append(exchange(sent[part], axis, gather_order(axis, part)[level]))
        if level:
            half = kept[0].shape[0] // 2
            sent = [have[half:] + more[half:] for have, more in zip(kept, got)]
            kept = [have[:half] + more[:half] for have, more in zip(kept, got)]
    return kept, got


def gram_sum(pieces, axis):
    held, near, own, far = [piece[-GRAM:].reshape(K // 2, TILE) for piece in pieces[0]]
    gram = (held + near) + (own + far)
    first, *rest = [gather_order(axis, 0)[-2:]] + gather_order(axis, 0)[:-2]
    others = []
    for bit in (first[0], first[1], first[0] | first[1]):
        others.append(exchange(gram, axis, bit))
    gram = (gram + others[0]) + (others[1] + others[2])
    for bit in rest:
        other = exchange(gram, axis, bit)
        gram = gram + other
    return gram


def all_sum(value):
    for axis in ("items", "users"):
        for bit in gather_order(axis, 0)[::-1]:
            value = value + exchange(value, axis, bit)
    return value


def part_places(axis, part, blocks):
    swapped = gather_order(axis, part) != gather_order(axis, 0)
    quarter = blocks // 4
    return [at * quarter for at in ((0, 2, 1, 3) if swapped else (0, 1, 2, 3))], quarter


def tiles_kernel(count, source, target, *refs, places_in, places_out):
    piece_refs, refs = [refs[4 * part : 4 * part + 4] for part in range(PARTS)], refs[4 * PARTS :]
    tile_ref, keep_refs, send_refs = refs[0], refs[1 : 1 + PARTS], refs[1 + PARTS : 1 + 2 * PARTS]
    pieces, total = refs[1 + 2 * PARTS :]
    step = pl.program_id(0)
    half_out = keep_refs[-1].shape[0]

    @pl.when(step == 0)
    def _():
        for part in range(PARTS):
            starts, quarter = places_in[part]
            band = slice(part * ROWS, (part + 1) * ROWS)
            for at, place in enumerate(starts):
                ref = piece_refs[part][at]

                def prepare(block, carry):
                    value = ref[block]
                    top = value.astype(jnp.bfloat16)
                    pieces[place + block, band, :TILE] = top
                    pieces[place + block, band, TILE:] = (value - top.astype(jnp.float32)).astype(jnp.bfloat16)
                    return carry

                lax.fori_loop(0, quarter, prepare, 0, unroll=4)

        def clear(at, carry):
            total[at] = jnp.zeros((K, TILE), jnp.float32)
            return carry

        lax.fori_loop(0, 2 * half_out, clear, 0, unroll=4)

    live = jnp.clip(count[0] - step * BATCH, 0, BATCH)

    def group(at, carry):
        first = at * UNROLL
        products = []
        for slot in range(UNROLL):
            tile = tile_ref[first + slot]
            products.append(
                lax.dot_general(
                    pieces[source[step * BATCH + first + slot]],
                    jnp.concatenate([tile, tile], axis=0),
                    (((1,), (0,)), ((), ())),
                    preferred_element_type=jnp.float32,
                )
            )
        for slot in range(UNROLL):
            total[target[step * BATCH + first + slot]] += products[slot]
        return carry

    lax.fori_loop(0, (live + UNROLL - 1) // UNROLL, group, 0)

    @pl.when(step == pl.num_programs(0) - 1)
    def _():
        for part in range(PARTS):
            starts, quarter = places_out[part]
            band = slice(part * ROWS, (part + 1) * ROWS)
            for at, place in enumerate(starts):
                ref = (keep_refs, keep_refs, send_refs, send_refs)[at][part]
                first = at % 2 * quarter

                def finish(block, carry):
                    ref[first + block] = total[place + block, band]
                    return carry

                lax.fori_loop(0, quarter, finish, 0, unroll=4)


def tiles_product(count, source, target, pieces, tiles, blocks_out, axis_in, axis_out):
    quarter_in = pieces[-1][0].shape[0]
    half_out = blocks_out // 2

    def tile_block(step, count, source, target):
        return (jnp.minimum(step, (count[0] + BATCH - 1) // BATCH - 1), 0, 0)

    kernel = functools.partial(
        tiles_kernel,
        places_in=[part_places(axis_in, part, 4 * quarter_in) for part in range(PARTS)],
        places_out=[part_places(axis_out, part, 2 * half_out) for part in range(PARTS)],
    )
    call = pl.pallas_call(
        kernel,
        out_shape=[jax.ShapeDtypeStruct((half_out, ROWS, TILE), jnp.float32)] * (2 * PARTS),
        grid_spec=pltpu.PrefetchScalarGridSpec(
            num_scalar_prefetch=3,
            grid=(tiles.shape[0] // BATCH,),
            in_specs=[VMEM_SPEC] * (4 * PARTS)
            + [pl.BlockSpec((BATCH, TILE, TILE), tile_block)],
            out_specs=[VMEM_SPEC] * (2 * PARTS),
            scratch_shapes=[
                pltpu.VMEM((4 * quarter_in, K, 2 * TILE), jnp.bfloat16),
                pltpu.VMEM((2 * half_out + 1, K, TILE), jnp.float32),
            ],
        ),
    )
    out = call(count, source, target, *[piece for part in pieces for piece in part], tiles)
    return out[:PARTS], out[PARTS:]


def dot_full(left, right, contract):
    return lax.dot_general(
        left, right, ((contract[:1], contract[1:]), ((), ())), precision=HIGHEST, preferred_element_type=jnp.float32
    )


def factor_kernel(gram_ref, out_ref, *, total):
    row = lax.broadcasted_iota(jnp.int32, (K, K), 0)
    col = lax.broadcasted_iota(jnp.int32, (K, K), 1)
    gram = jnp.concatenate([gram_ref[:, :K], gram_ref[:, K:]], axis=0) * (1.0 / total)
    work = jnp.concatenate([gram, (row == col).astype(jnp.float32)], axis=1)
    bands = [work[8 * at : 8 * at + 8] for at in range(K // 8)]
    place = lax.broadcasted_iota(jnp.int32, (8, 1), 0)
    for at in range(K):
        band, inside = divmod(at, 8)
        pivot_row = bands[band][inside : inside + 1, :]
        inverse = 1.0 / pivot_row[:, at : at + 1]
        for under in range(band, K // 8):
            factor = bands[under][:, at : at + 1] * inverse
            if under == band:
                factor = jnp.where(place > inside, factor, 0.0)
            bands[under] = bands[under] - factor * pivot_row
    work = jnp.concatenate(bands, axis=0)
    pivots = jnp.sum(jnp.where(row == col, work[:, :K], 0.0), axis=1, keepdims=True)
    out_ref[...] = work[:, K:] * lax.rsqrt(pivots)


def turn_kernel(tile_ref, *refs):
    out_ref = refs[-1]
    for at in range(tile_ref.shape[0]):
        out_ref[at] = tile_ref[at].T


def turned_tiles(tiles, first, blocks, into):
    size = tiles.shape[0] // 16
    block = pl.BlockSpec((size, TILE, TILE), lambda step: (step + first, 0, 0))
    return pl.pallas_call(
        turn_kernel,
        out_shape=jax.ShapeDtypeStruct(tiles.shape, tiles.dtype),
        grid=(blocks,),
        in_specs=[block] + ([] if into is None else [pl.BlockSpec(memory_space=pl.ANY)]),
        out_specs=block,
        input_output_aliases={} if into is None else {1: 0},
        name="turned_tiles",
    )(*([tiles] if into is None else [tiles, into]))


def inverse_factor(gram, total):
    return pl.pallas_call(
        functools.partial(factor_kernel, total=total),
        out_shape=jax.ShapeDtypeStruct((K, K), jnp.float32),
        in_specs=[VMEM_SPEC],
        out_specs=VMEM_SPEC,
        name="factor",
    )(gram)


def scale_kernel(*refs, factored):
    refs = list(refs)
    inverse = refs.pop(0)[...] if factored else None
    raw_refs, refs = list(zip(refs[:PARTS], refs[PARTS : 2 * PARTS])), refs[2 * PARTS :]
    scale_ref, panel_ref, sent_refs = refs[0], refs[1], refs[2:]
    blocks = scale_ref.shape[0]
    gram = jnp.zeros((K, K), jnp.float32)
    for at in range(blocks):
        scale = scale_ref[at][None, :]
        panel = jnp.concatenate([kept[at] + got[at] for kept, got in raw_refs], axis=0)
        if factored:
            panel = dot_full(inverse, panel, (1, 0))
        panel = scale * panel
        panel_ref[at] = panel
        for part in range(PARTS):
            sent_refs[part][at] = scale * panel[part * ROWS : (part + 1) * ROWS]
        gram = gram + dot_full(panel, panel, (1, 1))
    gram = jnp.concatenate([gram[: K // 2], gram[K // 2 :]], axis=1)
    for at in range(GRAM):
        sent_refs[0][blocks + at] = gram[at * ROWS : (at + 1) * ROWS]


def scale_panel(inverse, kept, got, scale):
    factored = inverse is not None
    operands = ([inverse] if factored else []) + list(kept) + list(got) + [scale]
    blocks = scale.shape[0]
    panel, *sent = pl.pallas_call(
        functools.partial(scale_kernel, factored=factored),
        out_shape=[jax.ShapeDtypeStruct((blocks, K, TILE), jnp.float32)]
        + [jax.ShapeDtypeStruct((blocks + GRAM * (part == 0), ROWS, TILE), jnp.float32) for part in range(PARTS)],
        in_specs=[VMEM_SPEC] * len(operands),
        out_specs=[VMEM_SPEC] * (1 + PARTS),
        name="scale_panel",
    )(*operands)
    return panel, sent


def finish_kernel(inverse_ref, panel_ref, out_ref):
    for at in range(panel_ref.shape[0]):
        out_ref[:, at * TILE : (at + 1) * TILE] = dot_full(inverse_ref[...], panel_ref[at], (1, 0))


def finish_panel(inverse, panel):
    return pl.pallas_call(
        finish_kernel,
        out_shape=jax.ShapeDtypeStruct((K, panel.shape[0] * TILE), jnp.float32),
        in_specs=[VMEM_SPEC] * 2,
        out_specs=VMEM_SPEC,
        name="finish_panel",
    )(inverse, panel)


def body(tile_rows, tile_cols, tile_count, tile_vals, user_degree, item_degree, start_items):
    user_groups = lax.axis_size("users")
    item_groups = lax.axis_size("items")
    user_blocks = UT // item_groups
    item_blocks = IT // user_groups
    user_total = UT * TILE * user_groups
    item_total = IT * TILE * item_groups

    rows = tile_rows[0, 0]
    cols = tile_cols[0, 0]
    tiles = tile_vals[0, 0]
    count = tile_count[0]
    live = jnp.arange(rows.shape[0], dtype=jnp.int32) < count[0]
    row_at = relative_position(rows // user_blocks, "items", 0) * user_blocks + rows % user_blocks
    col_at = relative_position(cols // item_blocks, "users", 0) * item_blocks + cols % item_blocks
    row_to = jnp.where(live, row_at, UT)
    col_to = jnp.where(live, col_at, IT)

    user_scale = lax.rsqrt(user_degree.astype(jnp.float32)).reshape(user_blocks, TILE)
    item_scale = lax.rsqrt(item_degree.astype(jnp.float32)).reshape(item_blocks, TILE)
    start = start_items.astype(jnp.float32).reshape(PARTS, ROWS, item_blocks, TILE).transpose(0, 2, 1, 3)
    start = item_scale[None, :, None, :] * start
    sent = [start[part] for part in range(PARTS)]
    sent[0] = jnp.concatenate([sent[0], jnp.zeros((GRAM, ROWS, TILE), jnp.float32)], axis=0)
    turned = turned_tiles(tiles, 0, 8, None)
    turned = turned_tiles(tiles, 8, 8, turned)
    item_inverse = None
    for step in range(ITERS):
        pieces = gather(sent, "users")
        if step:
            item_inverse = inverse_factor(gram_sum(pieces, "items"), item_total)
        kept, out = tiles_product(count, col_at, row_to, pieces, turned, UT, "users", "items")
        kept, got = reduce_scatter(kept, out, "items")
        user_raw, sent = scale_panel(item_inverse, kept, got, user_scale)
        pieces = gather(sent, "items")
        user_inverse = inverse_factor(gram_sum(pieces, "users"), user_total)
        kept, out = tiles_product(count, row_at, col_to, pieces, tiles, IT, "items", "users")
        kept, got = reduce_scatter(kept, out, "users")
        if step == ITERS - 1:
            user_panel = finish_panel(user_inverse, user_raw)
            user_panel, got = lax.optimization_barrier((user_panel, got))
        item_raw, sent = scale_panel(user_inverse, kept, got, item_scale)
    item_inverse = inverse_factor(all_sum(sent[0][-GRAM:].reshape(K // 2, TILE)), item_total)
    return user_panel, finish_panel(item_inverse, item_raw)


def solution(mesh):
    in_specs = (
        P("users", "items", None),
        P("users", "items", None),
        P("users", "items"),
        P("users", "items", None, None, None),
        P(("users", "items")),
        P(("items", "users")),
        P(None, ("items", "users")),
    )
    out_specs = (P(None, ("users", "items")), P(None, ("items", "users")))
    return jax.shard_map(body, mesh=mesh, in_specs=in_specs, out_specs=out_specs, check_vma=False)
```

```python
import functools

import jax
import jax.numpy as jnp
from jax import lax
from jax.experimental import pallas as pl
from jax.experimental.pallas import tpu as pltpu
from jax.sharding import PartitionSpec as P


K = 64
PARTS = 4
ROWS = K // PARTS
TILE = 128
GRAM = K // 2 // ROWS
ITERS = 2
UT = 64
IT = 64
BATCH = 64
UNROLL = 64
HIGHEST = lax.Precision.HIGHEST
VMEM_SPEC = pl.BlockSpec(memory_space=pltpu.VMEM)
SMALL_KERNEL = pltpu.CompilerParams(vmem_limit_bytes=16 << 20)


def gather_order(axis, part):
    order = []
    bit = lax.axis_size(axis) >> 1
    while bit:
        order.append(bit)
        bit >>= 1
    if axis == "users" and part % 2 == 1:
        order[-2:] = order[-2:][::-1]
    return order


def exchange(value, axis, bit):
    return lax.ppermute(value, axis, [(at, at ^ bit) for at in range(lax.axis_size(axis))])


def relative_position(shard, axis, part):
    apart = shard ^ lax.axis_index(axis)
    place = jnp.zeros_like(apart)
    for level, bit in enumerate(gather_order(axis, part)):
        place = place + jnp.where(apart & bit != 0, 1 << level, 0)
    return place


def gather(held, axis):
    held = list(held)
    levels = len(gather_order(axis, 0))
    for level in range(levels - 2):
        got = []
        for part in range(PARTS):
            got.append(exchange(held[part], axis, gather_order(axis, part)[level]))
        first = jnp.concatenate([held[0][:-GRAM], got[0][:-GRAM], held[0][-GRAM:] + got[0][-GRAM:]], axis=0)
        held = [first] + [jnp.concatenate([have, more], axis=0) for have, more in zip(held[1:], got[1:])]
    order = [gather_order(axis, part)[-2:] for part in range(PARTS)]
    near, own, far = [], [], []
    for part in range(PARTS):
        near.append(exchange(held[part], axis, order[part][0]))
        own.append(exchange(held[part], axis, order[part][1]))
    for part in range(PARTS):
        far.append(exchange(near[part], axis, order[part][1]))
    return [[held[part], near[part], own[part], far[part]] for part in range(PARTS)]


def reduce_scatter(kept, sent, axis):
    for level in range(len(gather_order(axis, 0)) - 1, -1, -1):
        got = []
        for part in range(PARTS):
            got.append(exchange(sent[part], axis, gather_order(axis, part)[level]))
        if level:
            half = kept[0].shape[0] // 2
            sent = [have[half:] + more[half:] for have, more in zip(kept, got)]
            kept = [have[:half] + more[:half] for have, more in zip(kept, got)]
    return kept, got


def gram_sum(pieces, axis):
    held, near, own, far = [piece[-GRAM:].reshape(K // 2, TILE) for piece in pieces[0]]
    gram = (held + near) + (own + far)
    first, *rest = [gather_order(axis, 0)[-2:]] + gather_order(axis, 0)[:-2]
    others = []
    for bit in (first[0], first[1], first[0] | first[1]):
        others.append(exchange(gram, axis, bit))
    gram = (gram + others[0]) + (others[1] + others[2])
    for bit in rest:
        other = exchange(gram, axis, bit)
        gram = gram + other
    return gram


def all_sum(value):
    for axis in ("items", "users"):
        for bit in gather_order(axis, 0)[::-1]:
            value = value + exchange(value, axis, bit)
    return value


def part_places(axis, part, blocks):
    swapped = gather_order(axis, part) != gather_order(axis, 0)
    quarter = blocks // 4
    return [at * quarter for at in ((0, 2, 1, 3) if swapped else (0, 1, 2, 3))], quarter


def tiles_kernel(count, source, target, *refs, places_in, places_out):
    piece_refs, refs = [refs[4 * part : 4 * part + 4] for part in range(PARTS)], refs[4 * PARTS :]
    tile_ref, keep_refs, send_refs = refs[0], refs[1 : 1 + PARTS], refs[1 + PARTS : 1 + 2 * PARTS]
    pieces, total = refs[1 + 2 * PARTS :]
    step = pl.program_id(0)
    half_out = keep_refs[-1].shape[0]

    @pl.when(step == 0)
    def _():
        for part in range(PARTS):
            starts, quarter = places_in[part]
            band = slice(part * ROWS, (part + 1) * ROWS)
            for at, place in enumerate(starts):
                ref = piece_refs[part][at]

                def prepare(block, carry):
                    value = ref[block]
                    top = value.astype(jnp.bfloat16)
                    pieces[place + block, band, :TILE] = top
                    pieces[place + block, band, TILE:] = (value - top.astype(jnp.float32)).astype(jnp.bfloat16)
                    return carry

                lax.fori_loop(0, quarter, prepare, 0, unroll=4)

        def clear(at, carry):
            total[at] = jnp.zeros((K, TILE), jnp.float32)
            return carry

        lax.fori_loop(0, 2 * half_out, clear, 0, unroll=4)

    live = jnp.clip(count[0] - step * BATCH, 0, BATCH)

    def group(at, carry):
        first = at * UNROLL
        products = []
        for slot in range(UNROLL):
            tile = tile_ref[first + slot]
            products.append(
                lax.dot_general(
                    pieces[source[step * BATCH + first + slot]],
                    jnp.concatenate([tile, tile], axis=0),
                    (((1,), (0,)), ((), ())),
                    preferred_element_type=jnp.float32,
                )
            )
        for slot in range(UNROLL):
            total[target[step * BATCH + first + slot]] += products[slot]
        return carry

    lax.fori_loop(0, (live + UNROLL - 1) // UNROLL, group, 0)

    @pl.when(step == pl.num_programs(0) - 1)
    def _():
        for part in range(PARTS):
            starts, quarter = places_out[part]
            band = slice(part * ROWS, (part + 1) * ROWS)
            for at, place in enumerate(starts):
                ref = (keep_refs, keep_refs, send_refs, send_refs)[at][part]
                first = at % 2 * quarter

                def finish(block, carry):
                    ref[first + block] = total[place + block, band]
                    return carry

                lax.fori_loop(0, quarter, finish, 0, unroll=4)


def tiles_product(count, source, target, pieces, tiles, blocks_out, axis_in, axis_out):
    quarter_in = pieces[-1][0].shape[0]
    half_out = blocks_out // 2

    def tile_block(step, count, source, target):
        return (jnp.minimum(step, (count[0] + BATCH - 1) // BATCH - 1), 0, 0)

    kernel = functools.partial(
        tiles_kernel,
        places_in=[part_places(axis_in, part, 4 * quarter_in) for part in range(PARTS)],
        places_out=[part_places(axis_out, part, 2 * half_out) for part in range(PARTS)],
    )
    call = pl.pallas_call(
        kernel,
        out_shape=[pltpu.VMEM((half_out, ROWS, TILE), jnp.float32)] * (2 * PARTS),
        grid_spec=pltpu.PrefetchScalarGridSpec(
            num_scalar_prefetch=3,
            grid=(tiles.shape[0] // BATCH,),
            in_specs=[VMEM_SPEC] * (4 * PARTS)
            + [pl.BlockSpec((BATCH, TILE, TILE), tile_block)],
            out_specs=[VMEM_SPEC] * (2 * PARTS),
            scratch_shapes=[
                pltpu.VMEM((4 * quarter_in, K, 2 * TILE), jnp.bfloat16),
                pltpu.VMEM((2 * half_out + 1, K, TILE), jnp.float32),
            ],
        ),
        compiler_params=pltpu.CompilerParams(vmem_limit_bytes=20 << 20),
    )
    out = call(count, source, target, *[in_vmem(piece) for part in pieces for piece in part], tiles)
    return out[:PARTS], out[PARTS:]


def in_vmem(value):
    return pltpu.with_memory_space_constraint(value, pltpu.VMEM)


def dot_full(left, right, contract):
    return lax.dot_general(
        left, right, ((contract[:1], contract[1:]), ((), ())), precision=HIGHEST, preferred_element_type=jnp.float32
    )


def factor_kernel(gram_ref, out_ref, *, total):
    row = lax.broadcasted_iota(jnp.int32, (K, K), 0)
    col = lax.broadcasted_iota(jnp.int32, (K, K), 1)
    gram = jnp.concatenate([gram_ref[:, :K], gram_ref[:, K:]], axis=0) * (1.0 / total)
    work = jnp.concatenate([gram, (row == col).astype(jnp.float32)], axis=1)
    bands = [work[8 * at : 8 * at + 8] for at in range(K // 8)]
    place = lax.broadcasted_iota(jnp.int32, (8, 1), 0)
    for at in range(K):
        band, inside = divmod(at, 8)
        pivot_row = bands[band][inside : inside + 1, :]
        inverse = 1.0 / pivot_row[:, at : at + 1]
        for under in range(band, K // 8):
            factor = bands[under][:, at : at + 1] * inverse
            if under == band:
                factor = jnp.where(place > inside, factor, 0.0)
            bands[under] = bands[under] - factor * pivot_row
    work = jnp.concatenate(bands, axis=0)
    pivots = jnp.sum(jnp.where(row == col, work[:, :K], 0.0), axis=1, keepdims=True)
    out_ref[...] = work[:, K:] * lax.rsqrt(pivots)


def turn_kernel(tile_ref, *refs):
    out_ref = refs[-1]
    for at in range(tile_ref.shape[0]):
        out_ref[at] = tile_ref[at].T


def turned_tiles(tiles, first, blocks, into):
    size = tiles.shape[0] // 16
    block = pl.BlockSpec((size, TILE, TILE), lambda step: (step + first, 0, 0))
    return pl.pallas_call(
        turn_kernel,
        out_shape=jax.ShapeDtypeStruct(tiles.shape, tiles.dtype),
        grid=(blocks,),
        in_specs=[block] + ([] if into is None else [pl.BlockSpec(memory_space=pl.ANY)]),
        out_specs=block,
        compiler_params=SMALL_KERNEL,
        input_output_aliases={} if into is None else {1: 0},
        name="turned_tiles",
    )(*([tiles] if into is None else [tiles, into]))


def inverse_factor(gram, total):
    return pl.pallas_call(
        functools.partial(factor_kernel, total=total),
        out_shape=pltpu.VMEM((K, K), jnp.float32),
        in_specs=[VMEM_SPEC],
        out_specs=VMEM_SPEC,
        compiler_params=SMALL_KERNEL,
        name="factor",
    )(in_vmem(gram))


def scale_kernel(*refs, factored):
    refs = list(refs)
    inverse = refs.pop(0)[...] if factored else None
    raw_refs, refs = list(zip(refs[:PARTS], refs[PARTS : 2 * PARTS])), refs[2 * PARTS :]
    scale_ref, panel_ref, sent_refs = refs[0], refs[1], refs[2:]
    blocks = scale_ref.shape[0]
    gram = jnp.zeros((K, K), jnp.float32)
    for at in range(blocks):
        scale = scale_ref[at][None, :]
        panel = jnp.concatenate([kept[at] + got[at] for kept, got in raw_refs], axis=0)
        if factored:
            panel = dot_full(inverse, panel, (1, 0))
        panel = scale * panel
        panel_ref[at] = panel
        for part in range(PARTS):
            sent_refs[part][at] = scale * panel[part * ROWS : (part + 1) * ROWS]
        gram = gram + dot_full(panel, panel, (1, 1))
    gram = jnp.concatenate([gram[: K // 2], gram[K // 2 :]], axis=1)
    for at in range(GRAM):
        sent_refs[0][blocks + at] = gram[at * ROWS : (at + 1) * ROWS]


def scale_panel(inverse, kept, got, scale):
    factored = inverse is not None
    operands = ([inverse] if factored else []) + list(kept) + list(got) + [scale]
    blocks = scale.shape[0]
    panel, *sent = pl.pallas_call(
        functools.partial(scale_kernel, factored=factored),
        out_shape=[jax.ShapeDtypeStruct((blocks, K, TILE), jnp.float32)]
        + [pltpu.VMEM((blocks + GRAM * (part == 0), ROWS, TILE), jnp.float32) for part in range(PARTS)],
        in_specs=[VMEM_SPEC] * len(operands),
        out_specs=[VMEM_SPEC] * (1 + PARTS),
        compiler_params=SMALL_KERNEL,
        name="scale_panel",
    )(*map(in_vmem, operands))
    return panel, sent


def finish_kernel(inverse_ref, panel_ref, out_ref):
    for at in range(panel_ref.shape[0]):
        out_ref[:, at * TILE : (at + 1) * TILE] = dot_full(inverse_ref[...], panel_ref[at], (1, 0))


def finish_panel(inverse, panel):
    return pl.pallas_call(
        finish_kernel,
        out_shape=jax.ShapeDtypeStruct((K, panel.shape[0] * TILE), jnp.float32),
        in_specs=[VMEM_SPEC] * 2,
        out_specs=VMEM_SPEC,
        compiler_params=SMALL_KERNEL,
        name="finish_panel",
    )(inverse, panel)


def body(tile_rows, tile_cols, tile_count, tile_vals, user_degree, item_degree, start_items):
    user_groups = lax.axis_size("users")
    item_groups = lax.axis_size("items")
    user_blocks = UT // item_groups
    item_blocks = IT // user_groups
    user_total = UT * TILE * user_groups
    item_total = IT * TILE * item_groups

    rows = tile_rows[0, 0]
    cols = tile_cols[0, 0]
    tiles = tile_vals[0, 0]
    count = tile_count[0]
    live = jnp.arange(rows.shape[0], dtype=jnp.int32) < count[0]
    row_at = relative_position(rows // user_blocks, "items", 0) * user_blocks + rows % user_blocks
    col_at = relative_position(cols // item_blocks, "users", 0) * item_blocks + cols % item_blocks
    row_to = jnp.where(live, row_at, UT)
    col_to = jnp.where(live, col_at, IT)

    user_scale = lax.rsqrt(user_degree.astype(jnp.float32)).reshape(user_blocks, TILE)
    item_scale = lax.rsqrt(item_degree.astype(jnp.float32)).reshape(item_blocks, TILE)
    start = start_items.astype(jnp.float32).reshape(PARTS, ROWS, item_blocks, TILE).transpose(0, 2, 1, 3)
    start = item_scale[None, :, None, :] * start
    sent = [start[part] for part in range(PARTS)]
    sent[0] = jnp.concatenate([sent[0], jnp.zeros((GRAM, ROWS, TILE), jnp.float32)], axis=0)
    turned = turned_tiles(tiles, 0, 8, None)
    turned = turned_tiles(tiles, 8, 8, turned)
    item_inverse = None
    for step in range(ITERS):
        pieces = gather(sent, "users")
        if step:
            item_inverse = inverse_factor(gram_sum(pieces, "items"), item_total)
        kept, out = tiles_product(count, col_at, row_to, pieces, turned, UT, "users", "items")
        kept, got = reduce_scatter(kept, out, "items")
        user_raw, sent = scale_panel(item_inverse, kept, got, user_scale)
        pieces = gather(sent, "items")
        user_inverse = inverse_factor(gram_sum(pieces, "users"), user_total)
        kept, out = tiles_product(count, row_at, col_to, pieces, tiles, IT, "items", "users")
        kept, got = reduce_scatter(kept, out, "users")
        if step == ITERS - 1:
            user_panel = finish_panel(user_inverse, user_raw)
            user_panel, got = lax.optimization_barrier((user_panel, got))
        item_raw, sent = scale_panel(user_inverse, kept, got, item_scale)
    item_inverse = inverse_factor(all_sum(sent[0][-GRAM:].reshape(K // 2, TILE)), item_total)
    return user_panel, finish_panel(item_inverse, item_raw)


def solution(mesh):
    in_specs = (
        P("users", "items", None),
        P("users", "items", None),
        P("users", "items"),
        P("users", "items", None, None, None),
        P(("users", "items")),
        P(("items", "users")),
        P(None, ("items", "users")),
    )
    out_specs = (P(None, ("users", "items")), P(None, ("items", "users")))
    return jax.shard_map(body, mesh=mesh, in_specs=in_specs, out_specs=out_specs, check_vma=False)
```

```python
import functools

import jax
import jax.numpy as jnp
from jax import lax
from jax.experimental import pallas as pl
from jax.experimental.pallas import tpu as pltpu
from jax.sharding import PartitionSpec as P


K = 64
PARTS = 4
ROWS = K // PARTS
TILE = 128
GRAM = K // 2 // ROWS
ITERS = 2
UT = 64
IT = 64
BATCH = 64
UNROLL = 64
HIGHEST = lax.Precision.HIGHEST
VMEM_SPEC = pl.BlockSpec(memory_space=pltpu.VMEM)
SMALL_KERNEL = pltpu.CompilerParams(vmem_limit_bytes=16 << 20)


def gather_order(axis, part):
    order = []
    bit = lax.axis_size(axis) >> 1
    while bit:
        order.append(bit)
        bit >>= 1
    if axis == "users" and part % 2 == 1:
        order[-2:] = order[-2:][::-1]
    return order


def exchange(value, axis, bit):
    return lax.ppermute(value, axis, [(at, at ^ bit) for at in range(lax.axis_size(axis))])


def relative_position(shard, axis, part):
    apart = shard ^ lax.axis_index(axis)
    place = jnp.zeros_like(apart)
    for level, bit in enumerate(gather_order(axis, part)):
        place = place + jnp.where(apart & bit != 0, 1 << level, 0)
    return place


def gather(held, axis):
    held = list(held)
    levels = len(gather_order(axis, 0))
    for level in range(levels - 2):
        got = []
        for part in range(PARTS):
            got.append(exchange(held[part], axis, gather_order(axis, part)[level]))
        first = jnp.concatenate([held[0][:-GRAM], got[0][:-GRAM], held[0][-GRAM:] + got[0][-GRAM:]], axis=0)
        held = [first] + [jnp.concatenate([have, more], axis=0) for have, more in zip(held[1:], got[1:])]
    order = [gather_order(axis, part)[-2:] for part in range(PARTS)]
    near, own, far = [], [], []
    for part in range(PARTS):
        near.append(exchange(held[part], axis, order[part][0]))
        own.append(exchange(held[part], axis, order[part][1]))
    for part in range(PARTS):
        far.append(exchange(near[part], axis, order[part][1]))
    return [[held[part], near[part], own[part], far[part]] for part in range(PARTS)]


def reduce_scatter(kept, sent, axis):
    for level in range(len(gather_order(axis, 0)) - 1, -1, -1):
        got = []
        for part in range(PARTS):
            got.append(exchange(sent[part], axis, gather_order(axis, part)[level]))
        if level:
            half = kept[0].shape[0] // 2
            sent = [have[half:] + more[half:] for have, more in zip(kept, got)]
            kept = [have[:half] + more[:half] for have, more in zip(kept, got)]
    return kept, got


def gram_sum(pieces, axis):
    held, near, own, far = [piece[-GRAM:].reshape(K // 2, TILE) for piece in pieces[0]]
    gram = (held + near) + (own + far)
    first, *rest = [gather_order(axis, 0)[-2:]] + gather_order(axis, 0)[:-2]
    others = []
    for bit in (first[0], first[1], first[0] | first[1]):
        others.append(exchange(gram, axis, bit))
    gram = (gram + others[0]) + (others[1] + others[2])
    for bit in rest:
        other = exchange(gram, axis, bit)
        gram = gram + other
    return gram


def all_sum(value):
    for axis in ("items", "users"):
        for bit in gather_order(axis, 0)[::-1]:
            value = value + exchange(value, axis, bit)
    return value


def part_places(axis, part, blocks):
    swapped = gather_order(axis, part) != gather_order(axis, 0)
    quarter = blocks // 4
    return [at * quarter for at in ((0, 2, 1, 3) if swapped else (0, 1, 2, 3))], quarter


def tiles_kernel(count, source, target, *refs, places_in, places_out):
    piece_refs, refs = [refs[4 * part : 4 * part + 4] for part in range(PARTS)], refs[4 * PARTS :]
    tile_ref, keep_refs, send_refs = refs[0], refs[1 : 1 + PARTS], refs[1 + PARTS : 1 + 2 * PARTS]
    pieces, total = refs[1 + 2 * PARTS :]
    step = pl.program_id(0)
    half_out = keep_refs[-1].shape[0]

    @pl.when(step == 0)
    def _():
        for part in range(PARTS):
            starts, quarter = places_in[part]
            band = slice(part * ROWS, (part + 1) * ROWS)
            for at, place in enumerate(starts):
                ref = piece_refs[part][at]

                def prepare(block, carry):
                    value = ref[block]
                    top = value.astype(jnp.bfloat16)
                    pieces[place + block, band, :TILE] = top
                    pieces[place + block, band, TILE:] = (value - top.astype(jnp.float32)).astype(jnp.bfloat16)
                    return carry

                lax.fori_loop(0, quarter, prepare, 0, unroll=4)

        def clear(at, carry):
            total[at] = jnp.zeros((K, TILE), jnp.float32)
            return carry

        lax.fori_loop(0, 2 * half_out, clear, 0, unroll=4)

    live = jnp.clip(count[0] - step * BATCH, 0, BATCH)

    def group(at, carry):
        first = at * UNROLL
        products = []
        for slot in range(UNROLL):
            tile = tile_ref[first + slot]
            products.append(
                lax.dot_general(
                    pieces[source[step * BATCH + first + slot]],
                    jnp.concatenate([tile, tile], axis=0),
                    (((1,), (0,)), ((), ())),
                    preferred_element_type=jnp.float32,
                )
            )
        for slot in range(UNROLL):
            total[target[step * BATCH + first + slot]] += products[slot]
        return carry

    lax.fori_loop(0, (live + UNROLL - 1) // UNROLL, group, 0)

    @pl.when(step == pl.num_programs(0) - 1)
    def _():
        for part in range(PARTS):
            starts, quarter = places_out[part]
            band = slice(part * ROWS, (part + 1) * ROWS)
            for at, place in enumerate(starts):
                ref = (keep_refs, keep_refs, send_refs, send_refs)[at][part]
                first = at % 2 * quarter

                def finish(block, carry):
                    ref[first + block] = total[place + block, band]
                    return carry

                lax.fori_loop(0, quarter, finish, 0, unroll=4)


def tiles_product(count, source, target, pieces, tiles, blocks_out, axis_in, axis_out):
    quarter_in = pieces[-1][0].shape[0]
    half_out = blocks_out // 2

    def tile_block(step, count, source, target):
        return (jnp.minimum(step, (count[0] + BATCH - 1) // BATCH - 1), 0, 0)

    kernel = functools.partial(
        tiles_kernel,
        places_in=[part_places(axis_in, part, 4 * quarter_in) for part in range(PARTS)],
        places_out=[part_places(axis_out, part, 2 * half_out) for part in range(PARTS)],
    )
    call = pl.pallas_call(
        kernel,
        out_shape=[pltpu.VMEM((half_out, ROWS, TILE), jnp.float32)] * (2 * PARTS),
        grid_spec=pltpu.PrefetchScalarGridSpec(
            num_scalar_prefetch=3,
            grid=(tiles.shape[0] // BATCH,),
            in_specs=[VMEM_SPEC] * (4 * PARTS)
            + [pl.BlockSpec((BATCH, TILE, TILE), tile_block)],
            out_specs=[VMEM_SPEC] * (2 * PARTS),
            scratch_shapes=[
                pltpu.VMEM((4 * quarter_in, K, 2 * TILE), jnp.bfloat16),
                pltpu.VMEM((2 * half_out + 1, K, TILE), jnp.float32),
            ],
        ),
        compiler_params=pltpu.CompilerParams(vmem_limit_bytes=20 << 20),
    )
    out = call(count, source, target, *[in_vmem(piece) for part in pieces for piece in part], tiles)
    return out[:PARTS], out[PARTS:]


def in_vmem(value):
    return pltpu.with_memory_space_constraint(value, pltpu.VMEM)


def dot_full(left, right, contract):
    return lax.dot_general(
        left, right, ((contract[:1], contract[1:]), ((), ())), precision=HIGHEST, preferred_element_type=jnp.float32
    )


def factor_kernel(gram_ref, out_ref, *, total):
    row = lax.broadcasted_iota(jnp.int32, (K, K), 0)
    col = lax.broadcasted_iota(jnp.int32, (K, K), 1)
    gram = jnp.concatenate([gram_ref[:, :K], gram_ref[:, K:]], axis=0) * (1.0 / total)
    work = jnp.concatenate([gram, (row == col).astype(jnp.float32)], axis=1)
    bands = [work[8 * at : 8 * at + 8] for at in range(K // 8)]
    place = lax.broadcasted_iota(jnp.int32, (8, 1), 0)
    for at in range(K):
        band, inside = divmod(at, 8)
        pivot_row = bands[band][inside : inside + 1, :]
        inverse = 1.0 / pivot_row[:, at : at + 1]
        for under in range(band, K // 8):
            factor = bands[under][:, at : at + 1] * inverse
            if under == band:
                factor = jnp.where(place > inside, factor, 0.0)
            bands[under] = bands[under] - factor * pivot_row
    work = jnp.concatenate(bands, axis=0)
    pivots = jnp.sum(jnp.where(row == col, work[:, :K], 0.0), axis=1, keepdims=True)
    out_ref[...] = work[:, K:] * lax.rsqrt(pivots)


def turn_kernel(tile_ref, out_ref):
    for at in range(tile_ref.shape[0]):
        out_ref[at] = tile_ref[at].T


def turned_tiles(tiles):
    block = pl.BlockSpec((tiles.shape[0] // 16, TILE, TILE), lambda step: (step, 0, 0))
    return pl.pallas_call(
        turn_kernel,
        out_shape=pltpu.HBM(tiles.shape, tiles.dtype),
        grid=(16,),
        in_specs=[block],
        out_specs=block,
        compiler_params=SMALL_KERNEL,
        name="turned_tiles",
    )(in_vmem(tiles))


def inverse_factor(gram, total):
    return pl.pallas_call(
        functools.partial(factor_kernel, total=total),
        out_shape=pltpu.VMEM((K, K), jnp.float32),
        in_specs=[VMEM_SPEC],
        out_specs=VMEM_SPEC,
        compiler_params=SMALL_KERNEL,
        name="factor",
    )(in_vmem(gram))


def scale_kernel(*refs, factored):
    refs = list(refs)
    inverse = refs.pop(0)[...] if factored else None
    raw_refs, refs = list(zip(refs[:PARTS], refs[PARTS : 2 * PARTS])), refs[2 * PARTS :]
    scale_ref, panel_ref, sent_refs = refs[0], refs[1], refs[2:]
    blocks = scale_ref.shape[0]
    gram = jnp.zeros((K, K), jnp.float32)
    for at in range(blocks):
        scale = scale_ref[at][None, :]
        panel = jnp.concatenate([kept[at] + got[at] for kept, got in raw_refs], axis=0)
        if factored:
            panel = dot_full(inverse, panel, (1, 0))
        panel = scale * panel
        panel_ref[at] = panel
        for part in range(PARTS):
            sent_refs[part][at] = scale * panel[part * ROWS : (part + 1) * ROWS]
        gram = gram + dot_full(panel, panel, (1, 1))
    gram = jnp.concatenate([gram[: K // 2], gram[K // 2 :]], axis=1)
    for at in range(GRAM):
        sent_refs[0][blocks + at] = gram[at * ROWS : (at + 1) * ROWS]


def scale_panel(inverse, kept, got, scale):
    factored = inverse is not None
    operands = ([inverse] if factored else []) + list(kept) + list(got) + [scale]
    blocks = scale.shape[0]
    panel, *sent = pl.pallas_call(
        functools.partial(scale_kernel, factored=factored),
        out_shape=[jax.ShapeDtypeStruct((blocks, K, TILE), jnp.float32)]
        + [pltpu.VMEM((blocks + GRAM * (part == 0), ROWS, TILE), jnp.float32) for part in range(PARTS)],
        in_specs=[VMEM_SPEC] * len(operands),
        out_specs=[VMEM_SPEC] * (1 + PARTS),
        compiler_params=SMALL_KERNEL,
        name="scale_panel",
    )(*map(in_vmem, operands))
    return panel, sent


def finish_kernel(inverse_ref, panel_ref, out_ref):
    for at in range(panel_ref.shape[0]):
        out_ref[:, at * TILE : (at + 1) * TILE] = dot_full(inverse_ref[...], panel_ref[at], (1, 0))


def finish_panel(inverse, panel):
    return pl.pallas_call(
        finish_kernel,
        out_shape=jax.ShapeDtypeStruct((K, panel.shape[0] * TILE), jnp.float32),
        in_specs=[VMEM_SPEC] * 2,
        out_specs=VMEM_SPEC,
        compiler_params=SMALL_KERNEL,
        name="finish_panel",
    )(inverse, panel)


def body(tile_rows, tile_cols, tile_count, tile_vals, user_degree, item_degree, start_items):
    user_groups = lax.axis_size("users")
    item_groups = lax.axis_size("items")
    user_blocks = UT // item_groups
    item_blocks = IT // user_groups
    user_total = UT * TILE * user_groups
    item_total = IT * TILE * item_groups

    rows = tile_rows[0, 0]
    cols = tile_cols[0, 0]
    tiles = tile_vals[0, 0]
    count = tile_count[0]
    live = jnp.arange(rows.shape[0], dtype=jnp.int32) < count[0]
    row_at = relative_position(rows // user_blocks, "items", 0) * user_blocks + rows % user_blocks
    col_at = relative_position(cols // item_blocks, "users", 0) * item_blocks + cols % item_blocks
    row_to = jnp.where(live, row_at, UT)
    col_to = jnp.where(live, col_at, IT)

    user_scale = lax.rsqrt(user_degree.astype(jnp.float32)).reshape(user_blocks, TILE)
    item_scale = lax.rsqrt(item_degree.astype(jnp.float32)).reshape(item_blocks, TILE)
    start = start_items.astype(jnp.float32).reshape(PARTS, ROWS, item_blocks, TILE).transpose(0, 2, 1, 3)
    start = item_scale[None, :, None, :] * start
    sent = [start[part] for part in range(PARTS)]
    sent[0] = jnp.concatenate([sent[0], jnp.zeros((GRAM, ROWS, TILE), jnp.float32)], axis=0)
    turned = turned_tiles(tiles)
    item_inverse = None
    for step in range(ITERS):
        pieces = gather(sent, "users")
        if step:
            item_inverse = inverse_factor(gram_sum(pieces, "items"), item_total)
        source = turned if step else pltpu.with_memory_space_constraint(turned, pltpu.HBM)
        kept, out = tiles_product(count, col_at, row_to, pieces, source, UT, "users", "items")
        kept, got = reduce_scatter(kept, out, "items")
        user_raw, sent = scale_panel(item_inverse, kept, got, user_scale)
        pieces = gather(sent, "items")
        user_inverse = inverse_factor(gram_sum(pieces, "users"), user_total)
        kept, out = tiles_product(count, row_at, col_to, pieces, tiles, IT, "items", "users")
        kept, got = reduce_scatter(kept, out, "users")
        if step == ITERS - 1:
            user_panel = finish_panel(user_inverse, user_raw)
            user_panel, got = lax.optimization_barrier((user_panel, got))
        item_raw, sent = scale_panel(user_inverse, kept, got, item_scale)
    item_inverse = inverse_factor(all_sum(sent[0][-GRAM:].reshape(K // 2, TILE)), item_total)
    return user_panel, finish_panel(item_inverse, item_raw)


def solution(mesh):
    in_specs = (
        P("users", "items", None),
        P("users", "items", None),
        P("users", "items"),
        P("users", "items", None, None, None),
        P(("users", "items")),
        P(("items", "users")),
        P(None, ("items", "users")),
    )
    out_specs = (P(None, ("users", "items")), P(None, ("items", "users")))
    return jax.shard_map(body, mesh=mesh, in_specs=in_specs, out_specs=out_specs, check_vma=False)
```

```python
import functools

import jax
import jax.numpy as jnp
from jax import lax
from jax.experimental import pallas as pl
from jax.experimental.pallas import tpu as pltpu
from jax.sharding import PartitionSpec as P


K = 64
PARTS = 4
ROWS = K // PARTS
TILE = 128
GRAM = K // 2 // ROWS
ITERS = 2
UT = 64
IT = 64
BATCH = 64
UNROLL = 64
HIGHEST = lax.Precision.HIGHEST
VMEM_SPEC = pl.BlockSpec(memory_space=pltpu.VMEM)
SMALL_KERNEL = pltpu.CompilerParams(vmem_limit_bytes=16 << 20)


def gather_order(axis, part):
    order = []
    bit = lax.axis_size(axis) >> 1
    while bit:
        order.append(bit)
        bit >>= 1
    if axis == "users" and part % 2 == 1:
        order[-2:] = order[-2:][::-1]
    return order


def exchange(value, axis, bit):
    return lax.ppermute(value, axis, [(at, at ^ bit) for at in range(lax.axis_size(axis))])


def relative_position(shard, axis, part):
    apart = shard ^ lax.axis_index(axis)
    place = jnp.zeros_like(apart)
    for level, bit in enumerate(gather_order(axis, part)):
        place = place + jnp.where(apart & bit != 0, 1 << level, 0)
    return place


def gather(held, axis):
    held = list(held)
    levels = len(gather_order(axis, 0))
    for level in range(levels - 2):
        got = []
        for part in range(PARTS):
            got.append(exchange(held[part], axis, gather_order(axis, part)[level]))
        first = jnp.concatenate([held[0][:-GRAM], got[0][:-GRAM], held[0][-GRAM:] + got[0][-GRAM:]], axis=0)
        held = [first] + [jnp.concatenate([have, more], axis=0) for have, more in zip(held[1:], got[1:])]
    order = [gather_order(axis, part)[-2:] for part in range(PARTS)]
    near, own, far = [], [], []
    for part in range(PARTS):
        near.append(exchange(held[part], axis, order[part][0]))
        own.append(exchange(held[part], axis, order[part][1]))
    for part in range(PARTS):
        far.append(exchange(near[part], axis, order[part][1]))
    return [[held[part], near[part], own[part], far[part]] for part in range(PARTS)]


def reduce_scatter(kept, sent, axis):
    for level in range(len(gather_order(axis, 0)) - 1, -1, -1):
        got = []
        for part in range(PARTS):
            got.append(exchange(sent[part], axis, gather_order(axis, part)[level]))
        if level:
            half = kept[0].shape[0] // 2
            sent = [have[half:] + more[half:] for have, more in zip(kept, got)]
            kept = [have[:half] + more[:half] for have, more in zip(kept, got)]
    return kept, got


def gram_sum(pieces, axis):
    held, near, own, far = [piece[-GRAM:].reshape(K // 2, TILE) for piece in pieces[0]]
    gram = (held + near) + (own + far)
    first, *rest = [gather_order(axis, 0)[-2:]] + gather_order(axis, 0)[:-2]
    others = []
    for bit in (first[0], first[1], first[0] | first[1]):
        others.append(exchange(gram, axis, bit))
    gram = (gram + others[0]) + (others[1] + others[2])
    for bit in rest:
        other = exchange(gram, axis, bit)
        gram = gram + other
    return gram


def all_sum(value):
    for axis in ("items", "users"):
        for bit in gather_order(axis, 0)[::-1]:
            value = value + exchange(value, axis, bit)
    return value


def part_places(axis, part, blocks):
    swapped = gather_order(axis, part) != gather_order(axis, 0)
    quarter = blocks // 4
    return [at * quarter for at in ((0, 2, 1, 3) if swapped else (0, 1, 2, 3))], quarter


def tiles_kernel(count, source, target, *refs, contract, places_in, places_out):
    piece_refs, refs = [refs[4 * part : 4 * part + 4] for part in range(PARTS)], refs[4 * PARTS :]
    tile_ref, keep_refs, send_refs = refs[0], refs[1 : 1 + PARTS], refs[1 + PARTS : 1 + 2 * PARTS]
    pieces, total = refs[1 + 2 * PARTS :]
    step = pl.program_id(0)
    half_out = keep_refs[-1].shape[0]

    @pl.when(step == 0)
    def _():
        for part in range(PARTS):
            starts, quarter = places_in[part]
            band = slice(part * ROWS, (part + 1) * ROWS)
            for at, place in enumerate(starts):
                ref = piece_refs[part][at]

                def prepare(block, carry):
                    value = ref[block]
                    top = value.astype(jnp.bfloat16)
                    pieces[place + block, band, :TILE] = top
                    pieces[place + block, band, TILE:] = (value - top.astype(jnp.float32)).astype(jnp.bfloat16)
                    return carry

                lax.fori_loop(0, quarter, prepare, 0, unroll=4)

        def clear(at, carry):
            total[at] = jnp.zeros((K, TILE), jnp.float32)
            return carry

        lax.fori_loop(0, 2 * half_out, clear, 0, unroll=4)

    live = jnp.clip(count[0] - step * BATCH, 0, BATCH)

    def group(at, carry):
        first = at * UNROLL
        products = []
        for slot in range(UNROLL):
            tile = tile_ref[first + slot]
            products.append(
                lax.dot_general(
                    pieces[source[step * BATCH + first + slot]],
                    jnp.concatenate([tile, tile], axis=contract),
                    (((1,), (contract,)), ((), ())),
                    preferred_element_type=jnp.float32,
                )
            )
        for slot in range(UNROLL):
            total[target[step * BATCH + first + slot]] += products[slot]
        return carry

    lax.fori_loop(0, (live + UNROLL - 1) // UNROLL, group, 0)

    @pl.when(step == pl.num_programs(0) - 1)
    def _():
        for part in range(PARTS):
            starts, quarter = places_out[part]
            band = slice(part * ROWS, (part + 1) * ROWS)
            for at, place in enumerate(starts):
                ref = (keep_refs, keep_refs, send_refs, send_refs)[at][part]
                first = at % 2 * quarter

                def finish(block, carry):
                    ref[first + block] = total[place + block, band]
                    return carry

                lax.fori_loop(0, quarter, finish, 0, unroll=4)


def tiles_product(count, source, target, pieces, tiles, blocks_out, axis_in, axis_out, contract):
    quarter_in = pieces[-1][0].shape[0]
    half_out = blocks_out // 2

    def tile_block(step, count, source, target):
        return (jnp.minimum(step, (count[0] + BATCH - 1) // BATCH - 1), 0, 0)

    kernel = functools.partial(
        tiles_kernel,
        contract=contract,
        places_in=[part_places(axis_in, part, 4 * quarter_in) for part in range(PARTS)],
        places_out=[part_places(axis_out, part, 2 * half_out) for part in range(PARTS)],
    )
    call = pl.pallas_call(
        kernel,
        out_shape=[pltpu.VMEM((half_out, ROWS, TILE), jnp.float32)] * (2 * PARTS),
        grid_spec=pltpu.PrefetchScalarGridSpec(
            num_scalar_prefetch=3,
            grid=(tiles.shape[0] // BATCH,),
            in_specs=[VMEM_SPEC] * (4 * PARTS)
            + [pl.BlockSpec((BATCH, TILE, TILE), tile_block)],
            out_specs=[VMEM_SPEC] * (2 * PARTS),
            scratch_shapes=[
                pltpu.VMEM((4 * quarter_in, K, 2 * TILE), jnp.bfloat16),
                pltpu.VMEM((2 * half_out + 1, K, TILE), jnp.float32),
            ],
        ),
        compiler_params=pltpu.CompilerParams(vmem_limit_bytes=20 << 20),
    )
    out = call(count, source, target, *[in_vmem(piece) for part in pieces for piece in part], tiles)
    return out[:PARTS], out[PARTS:]


def in_vmem(value):
    return pltpu.with_memory_space_constraint(value, pltpu.VMEM)


def dot_full(left, right, contract):
    return lax.dot_general(
        left, right, ((contract[:1], contract[1:]), ((), ())), precision=HIGHEST, preferred_element_type=jnp.float32
    )


def factor_kernel(gram_ref, out_ref, *, total):
    row = lax.broadcasted_iota(jnp.int32, (K, K), 0)
    col = lax.broadcasted_iota(jnp.int32, (K, K), 1)
    gram = jnp.concatenate([gram_ref[:, :K], gram_ref[:, K:]], axis=0) * (1.0 / total)
    work = jnp.concatenate([gram, (row == col).astype(jnp.float32)], axis=1)
    bands = [work[8 * at : 8 * at + 8] for at in range(K // 8)]
    place = lax.broadcasted_iota(jnp.int32, (8, 1), 0)
    for at in range(K):
        band, inside = divmod(at, 8)
        pivot_row = bands[band][inside : inside + 1, :]
        inverse = 1.0 / pivot_row[:, at : at + 1]
        for under in range(band, K // 8):
            factor = bands[under][:, at : at + 1] * inverse
            if under == band:
                factor = jnp.where(place > inside, factor, 0.0)
            bands[under] = bands[under] - factor * pivot_row
    work = jnp.concatenate(bands, axis=0)
    pivots = jnp.sum(jnp.where(row == col, work[:, :K], 0.0), axis=1, keepdims=True)
    out_ref[...] = work[:, K:] * lax.rsqrt(pivots)


def inverse_factor(gram, total):
    return pl.pallas_call(
        functools.partial(factor_kernel, total=total),
        out_shape=pltpu.VMEM((K, K), jnp.float32),
        in_specs=[VMEM_SPEC],
        out_specs=VMEM_SPEC,
        compiler_params=SMALL_KERNEL,
        name="factor",
    )(in_vmem(gram))


def scale_kernel(*refs, factored):
    refs = list(refs)
    inverse = refs.pop(0)[...] if factored else None
    raw_refs, refs = list(zip(refs[:PARTS], refs[PARTS : 2 * PARTS])), refs[2 * PARTS :]
    scale_ref, panel_ref, sent_refs = refs[0], refs[1], refs[2:]
    blocks = scale_ref.shape[0]
    gram = jnp.zeros((K, K), jnp.float32)
    for at in range(blocks):
        scale = scale_ref[at][None, :]
        panel = jnp.concatenate([kept[at] + got[at] for kept, got in raw_refs], axis=0)
        if factored:
            panel = dot_full(inverse, panel, (1, 0))
        panel = scale * panel
        panel_ref[at] = panel
        for part in range(PARTS):
            sent_refs[part][at] = scale * panel[part * ROWS : (part + 1) * ROWS]
        gram = gram + dot_full(panel, panel, (1, 1))
    gram = jnp.concatenate([gram[: K // 2], gram[K // 2 :]], axis=1)
    for at in range(GRAM):
        sent_refs[0][blocks + at] = gram[at * ROWS : (at + 1) * ROWS]


def scale_panel(inverse, kept, got, scale):
    factored = inverse is not None
    operands = ([inverse] if factored else []) + list(kept) + list(got) + [scale]
    blocks = scale.shape[0]
    panel, *sent = pl.pallas_call(
        functools.partial(scale_kernel, factored=factored),
        out_shape=[jax.ShapeDtypeStruct((blocks, K, TILE), jnp.float32)]
        + [pltpu.VMEM((blocks + GRAM * (part == 0), ROWS, TILE), jnp.float32) for part in range(PARTS)],
        in_specs=[VMEM_SPEC] * len(operands),
        out_specs=[VMEM_SPEC] * (1 + PARTS),
        compiler_params=SMALL_KERNEL,
        name="scale_panel",
    )(*map(in_vmem, operands))
    return panel, sent


def finish_kernel(inverse_ref, panel_ref, out_ref):
    for at in range(panel_ref.shape[0]):
        out_ref[:, at * TILE : (at + 1) * TILE] = dot_full(inverse_ref[...], panel_ref[at], (1, 0))


def finish_panel(inverse, panel):
    return pl.pallas_call(
        finish_kernel,
        out_shape=jax.ShapeDtypeStruct((K, panel.shape[0] * TILE), jnp.float32),
        in_specs=[VMEM_SPEC] * 2,
        out_specs=VMEM_SPEC,
        compiler_params=SMALL_KERNEL,
        name="finish_panel",
    )(inverse, panel)


def body(tile_rows, tile_cols, tile_count, tile_vals, user_degree, item_degree, start_items):
    user_groups = lax.axis_size("users")
    item_groups = lax.axis_size("items")
    user_blocks = UT // item_groups
    item_blocks = IT // user_groups
    user_total = UT * TILE * user_groups
    item_total = IT * TILE * item_groups

    rows = tile_rows[0, 0]
    cols = tile_cols[0, 0]
    tiles = tile_vals[0, 0]
    count = tile_count[0]
    live = jnp.arange(rows.shape[0], dtype=jnp.int32) < count[0]
    row_at = relative_position(rows // user_blocks, "items", 0) * user_blocks + rows % user_blocks
    col_at = relative_position(cols // item_blocks, "users", 0) * item_blocks + cols % item_blocks
    row_to = jnp.where(live, row_at, UT)
    col_to = jnp.where(live, col_at, IT)

    user_scale = lax.rsqrt(user_degree.astype(jnp.float32)).reshape(user_blocks, TILE)
    item_scale = lax.rsqrt(item_degree.astype(jnp.float32)).reshape(item_blocks, TILE)
    start = start_items.astype(jnp.float32).reshape(PARTS, ROWS, item_blocks, TILE).transpose(0, 2, 1, 3)
    start = item_scale[None, :, None, :] * start
    sent = [start[part] for part in range(PARTS)]
    sent[0] = jnp.concatenate([sent[0], jnp.zeros((GRAM, ROWS, TILE), jnp.float32)], axis=0)
    item_inverse = None
    for step in range(ITERS):
        pieces = gather(sent, "users")
        if step:
            item_inverse = inverse_factor(gram_sum(pieces, "items"), item_total)
        kept, out = tiles_product(count, col_at, row_to, pieces, tiles, UT, "users", "items", 1)
        kept, got = reduce_scatter(kept, out, "items")
        user_raw, sent = scale_panel(item_inverse, kept, got, user_scale)
        pieces = gather(sent, "items")
        user_inverse = inverse_factor(gram_sum(pieces, "users"), user_total)
        kept, out = tiles_product(count, row_at, col_to, pieces, tiles, IT, "items", "users", 0)
        kept, got = reduce_scatter(kept, out, "users")
        if step == ITERS - 1:
            user_panel = finish_panel(user_inverse, user_raw)
            user_panel, got = lax.optimization_barrier((user_panel, got))
        item_raw, sent = scale_panel(user_inverse, kept, got, item_scale)
    item_inverse = inverse_factor(all_sum(sent[0][-GRAM:].reshape(K // 2, TILE)), item_total)
    return user_panel, finish_panel(item_inverse, item_raw)


def solution(mesh):
    in_specs = (
        P("users", "items", None),
        P("users", "items", None),
        P("users", "items"),
        P("users", "items", None, None, None),
        P(("users", "items")),
        P(("items", "users")),
        P(None, ("items", "users")),
    )
    out_specs = (P(None, ("users", "items")), P(None, ("items", "users")))
    return jax.shard_map(body, mesh=mesh, in_specs=in_specs, out_specs=out_specs, check_vma=False)
```

```python
import functools

import jax
import jax.numpy as jnp
from jax import lax
from jax.experimental import pallas as pl
from jax.experimental.pallas import tpu as pltpu
from jax.sharding import PartitionSpec as P


K = 64
PARTS = 2
ROWS = K // PARTS
TILE = 128
GRAM = K // 2 // ROWS
ITERS = 2
UT = 64
IT = 64
BATCH = 64
UNROLL = 64
HIGHEST = lax.Precision.HIGHEST
VMEM_SPEC = pl.BlockSpec(memory_space=pltpu.VMEM)
SMALL_KERNEL = pltpu.CompilerParams(vmem_limit_bytes=16 << 20)


def gather_order(axis, part):
    order = []
    bit = lax.axis_size(axis) >> 1
    while bit:
        order.append(bit)
        bit >>= 1
    if axis == "users" and part % 2 == 1:
        order[-2:] = order[-2:][::-1]
    return order


def exchange(value, axis, bit):
    return lax.ppermute(value, axis, [(at, at ^ bit) for at in range(lax.axis_size(axis))])


def relative_position(shard, axis, part):
    apart = shard ^ lax.axis_index(axis)
    place = jnp.zeros_like(apart)
    for level, bit in enumerate(gather_order(axis, part)):
        place = place + jnp.where(apart & bit != 0, 1 << level, 0)
    return place


def gather(held, axis):
    held = list(held)
    levels = len(gather_order(axis, 0))
    for level in range(levels - 2):
        got = []
        for part in range(PARTS):
            got.append(exchange(held[part], axis, gather_order(axis, part)[level]))
        first = jnp.concatenate([held[0][:-GRAM], got[0][:-GRAM], held[0][-GRAM:] + got[0][-GRAM:]], axis=0)
        held = [first] + [jnp.concatenate([have, more], axis=0) for have, more in zip(held[1:], got[1:])]
    order = [gather_order(axis, part)[-2:] for part in range(PARTS)]
    near, own, far = [], [], []
    for part in range(PARTS):
        near.append(exchange(held[part], axis, order[part][0]))
        own.append(exchange(held[part], axis, order[part][1]))
    for part in range(PARTS):
        far.append(exchange(near[part], axis, order[part][1]))
    return [[held[part], near[part], own[part], far[part]] for part in range(PARTS)]


def reduce_scatter(kept, sent, axis):
    for level in range(len(gather_order(axis, 0)) - 1, -1, -1):
        got = []
        for part in range(PARTS):
            got.append(exchange(sent[part], axis, gather_order(axis, part)[level]))
        if level:
            half = kept[0].shape[0] // 2
            sent = [have[half:] + more[half:] for have, more in zip(kept, got)]
            kept = [have[:half] + more[:half] for have, more in zip(kept, got)]
    return kept, got


def gram_sum(pieces, axis):
    held, near, own, far = [piece[-GRAM:].reshape(K // 2, TILE) for piece in pieces[0]]
    gram = (held + near) + (own + far)
    first, *rest = [gather_order(axis, 0)[-2:]] + gather_order(axis, 0)[:-2]
    others = []
    for bit in (first[0], first[1], first[0] | first[1]):
        others.append(exchange(gram, axis, bit))
    gram = (gram + others[0]) + (others[1] + others[2])
    for bit in rest:
        other = exchange(gram, axis, bit)
        gram = gram + other
    return gram


def all_sum(value):
    for axis in ("items", "users"):
        for bit in gather_order(axis, 0)[::-1]:
            value = value + exchange(value, axis, bit)
    return value


def part_places(axis, part, blocks):
    swapped = gather_order(axis, part) != gather_order(axis, 0)
    quarter = blocks // 4
    return [at * quarter for at in ((0, 2, 1, 3) if swapped else (0, 1, 2, 3))], quarter


def tiles_kernel(count, source, target, *refs, contract, places_in, places_out):
    piece_refs, refs = [refs[4 * part : 4 * part + 4] for part in range(PARTS)], refs[4 * PARTS :]
    tile_ref, keep_refs, send_refs = refs[0], refs[1 : 1 + PARTS], refs[1 + PARTS : 1 + 2 * PARTS]
    pieces, total = refs[1 + 2 * PARTS :]
    step = pl.program_id(0)
    half_out = keep_refs[-1].shape[0]

    @pl.when(step == 0)
    def _():
        for part in range(PARTS):
            starts, quarter = places_in[part]
            band = slice(part * ROWS, (part + 1) * ROWS)
            for at, place in enumerate(starts):
                ref = piece_refs[part][at]

                def prepare(block, carry):
                    value = ref[block]
                    top = value.astype(jnp.bfloat16)
                    pieces[place + block, band, :TILE] = top
                    pieces[place + block, band, TILE:] = (value - top.astype(jnp.float32)).astype(jnp.bfloat16)
                    return carry

                lax.fori_loop(0, quarter, prepare, 0, unroll=4)

        def clear(at, carry):
            total[at] = jnp.zeros((K, TILE), jnp.float32)
            return carry

        lax.fori_loop(0, 2 * half_out, clear, 0, unroll=4)

    live = jnp.clip(count[0] - step * BATCH, 0, BATCH)

    def group(at, carry):
        first = at * UNROLL
        products = []
        for slot in range(UNROLL):
            tile = tile_ref[first + slot]
            products.append(
                lax.dot_general(
                    pieces[source[step * BATCH + first + slot]],
                    jnp.concatenate([tile, tile], axis=contract),
                    (((1,), (contract,)), ((), ())),
                    preferred_element_type=jnp.float32,
                )
            )
        for slot in range(UNROLL):
            total[target[step * BATCH + first + slot]] += products[slot]
        return carry

    lax.fori_loop(0, (live + UNROLL - 1) // UNROLL, group, 0)

    @pl.when(step == pl.num_programs(0) - 1)
    def _():
        for part in range(PARTS):
            starts, quarter = places_out[part]
            band = slice(part * ROWS, (part + 1) * ROWS)
            for at, place in enumerate(starts):
                ref = (keep_refs, keep_refs, send_refs, send_refs)[at][part]
                first = at % 2 * quarter

                def finish(block, carry):
                    ref[first + block] = total[place + block, band]
                    return carry

                lax.fori_loop(0, quarter, finish, 0, unroll=4)


def tiles_product(count, source, target, pieces, tiles, blocks_out, axis_in, axis_out, contract):
    quarter_in = pieces[-1][0].shape[0]
    half_out = blocks_out // 2

    def tile_block(step, count, source, target):
        return (jnp.minimum(step, (count[0] + BATCH - 1) // BATCH - 1), 0, 0)

    kernel = functools.partial(
        tiles_kernel,
        contract=contract,
        places_in=[part_places(axis_in, part, 4 * quarter_in) for part in range(PARTS)],
        places_out=[part_places(axis_out, part, 2 * half_out) for part in range(PARTS)],
    )
    call = pl.pallas_call(
        kernel,
        out_shape=[pltpu.VMEM((half_out, ROWS, TILE), jnp.float32)] * (2 * PARTS),
        grid_spec=pltpu.PrefetchScalarGridSpec(
            num_scalar_prefetch=3,
            grid=(tiles.shape[0] // BATCH,),
            in_specs=[VMEM_SPEC] * (4 * PARTS)
            + [pl.BlockSpec((BATCH, TILE, TILE), tile_block)],
            out_specs=[VMEM_SPEC] * (2 * PARTS),
            scratch_shapes=[
                pltpu.VMEM((4 * quarter_in, K, 2 * TILE), jnp.bfloat16),
                pltpu.VMEM((2 * half_out + 1, K, TILE), jnp.float32),
            ],
        ),
        compiler_params=pltpu.CompilerParams(vmem_limit_bytes=20 << 20),
    )
    out = call(count, source, target, *[in_vmem(piece) for part in pieces for piece in part], tiles)
    return out[:PARTS], out[PARTS:]


def in_vmem(value):
    return pltpu.with_memory_space_constraint(value, pltpu.VMEM)


def dot_full(left, right, contract):
    return lax.dot_general(
        left, right, ((contract[:1], contract[1:]), ((), ())), precision=HIGHEST, preferred_element_type=jnp.float32
    )


def factor_kernel(gram_ref, out_ref, *, total):
    row = lax.broadcasted_iota(jnp.int32, (K, K), 0)
    col = lax.broadcasted_iota(jnp.int32, (K, K), 1)
    gram = jnp.concatenate([gram_ref[:, :K], gram_ref[:, K:]], axis=0) * (1.0 / total)
    work = jnp.concatenate([gram, (row == col).astype(jnp.float32)], axis=1)
    bands = [work[8 * at : 8 * at + 8] for at in range(K // 8)]
    place = lax.broadcasted_iota(jnp.int32, (8, 1), 0)
    for at in range(K):
        band, inside = divmod(at, 8)
        pivot_row = bands[band][inside : inside + 1, :]
        inverse = 1.0 / pivot_row[:, at : at + 1]
        for under in range(band, K // 8):
            factor = bands[under][:, at : at + 1] * inverse
            if under == band:
                factor = jnp.where(place > inside, factor, 0.0)
            bands[under] = bands[under] - factor * pivot_row
    work = jnp.concatenate(bands, axis=0)
    pivots = jnp.sum(jnp.where(row == col, work[:, :K], 0.0), axis=1, keepdims=True)
    out_ref[...] = work[:, K:] * lax.rsqrt(pivots)


def inverse_factor(gram, total):
    return pl.pallas_call(
        functools.partial(factor_kernel, total=total),
        out_shape=pltpu.VMEM((K, K), jnp.float32),
        in_specs=[VMEM_SPEC],
        out_specs=VMEM_SPEC,
        compiler_params=SMALL_KERNEL,
        name="factor",
    )(in_vmem(gram))


def scale_kernel(*refs, factored):
    refs = list(refs)
    inverse = refs.pop(0)[...] if factored else None
    raw_refs, refs = list(zip(refs[:PARTS], refs[PARTS : 2 * PARTS])), refs[2 * PARTS :]
    scale_ref, panel_ref, sent_refs = refs[0], refs[1], refs[2:]
    blocks = scale_ref.shape[0]
    gram = jnp.zeros((K, K), jnp.float32)
    for at in range(blocks):
        scale = scale_ref[at][None, :]
        panel = jnp.concatenate([kept[at] + got[at] for kept, got in raw_refs], axis=0)
        if factored:
            panel = dot_full(inverse, panel, (1, 0))
        panel = scale * panel
        panel_ref[at] = panel
        for part in range(PARTS):
            sent_refs[part][at] = scale * panel[part * ROWS : (part + 1) * ROWS]
        gram = gram + dot_full(panel, panel, (1, 1))
    gram = jnp.concatenate([gram[: K // 2], gram[K // 2 :]], axis=1)
    for at in range(GRAM):
        sent_refs[0][blocks + at] = gram[at * ROWS : (at + 1) * ROWS]


def scale_panel(inverse, kept, got, scale):
    factored = inverse is not None
    operands = ([inverse] if factored else []) + list(kept) + list(got) + [scale]
    blocks = scale.shape[0]
    panel, *sent = pl.pallas_call(
        functools.partial(scale_kernel, factored=factored),
        out_shape=[jax.ShapeDtypeStruct((blocks, K, TILE), jnp.float32)]
        + [pltpu.VMEM((blocks + GRAM * (part == 0), ROWS, TILE), jnp.float32) for part in range(PARTS)],
        in_specs=[VMEM_SPEC] * len(operands),
        out_specs=[VMEM_SPEC] * (1 + PARTS),
        compiler_params=SMALL_KERNEL,
        name="scale_panel",
    )(*map(in_vmem, operands))
    return panel, sent


def finish_kernel(inverse_ref, panel_ref, out_ref):
    for at in range(panel_ref.shape[0]):
        out_ref[:, at * TILE : (at + 1) * TILE] = dot_full(inverse_ref[...], panel_ref[at], (1, 0))


def finish_panel(inverse, panel):
    return pl.pallas_call(
        finish_kernel,
        out_shape=jax.ShapeDtypeStruct((K, panel.shape[0] * TILE), jnp.float32),
        in_specs=[VMEM_SPEC] * 2,
        out_specs=VMEM_SPEC,
        compiler_params=SMALL_KERNEL,
        name="finish_panel",
    )(inverse, panel)


def body(tile_rows, tile_cols, tile_count, tile_vals, user_degree, item_degree, start_items):
    user_groups = lax.axis_size("users")
    item_groups = lax.axis_size("items")
    user_blocks = UT // item_groups
    item_blocks = IT // user_groups
    user_total = UT * TILE * user_groups
    item_total = IT * TILE * item_groups

    rows = tile_rows[0, 0]
    cols = tile_cols[0, 0]
    tiles = tile_vals[0, 0]
    count = tile_count[0]
    live = jnp.arange(rows.shape[0], dtype=jnp.int32) < count[0]
    row_at = relative_position(rows // user_blocks, "items", 0) * user_blocks + rows % user_blocks
    col_at = relative_position(cols // item_blocks, "users", 0) * item_blocks + cols % item_blocks
    row_to = jnp.where(live, row_at, UT)
    col_to = jnp.where(live, col_at, IT)

    user_scale = lax.rsqrt(user_degree.astype(jnp.float32)).reshape(user_blocks, TILE)
    item_scale = lax.rsqrt(item_degree.astype(jnp.float32)).reshape(item_blocks, TILE)
    start = start_items.astype(jnp.float32).reshape(PARTS, ROWS, item_blocks, TILE).transpose(0, 2, 1, 3)
    start = item_scale[None, :, None, :] * start
    sent = [start[part] for part in range(PARTS)]
    sent[0] = jnp.concatenate([sent[0], jnp.zeros((GRAM, ROWS, TILE), jnp.float32)], axis=0)
    item_inverse = None
    for step in range(ITERS):
        pieces = gather(sent, "users")
        if step:
            item_inverse = inverse_factor(gram_sum(pieces, "items"), item_total)
        source = tiles if step else pltpu.with_memory_space_constraint(tiles, pltpu.HBM)
        kept, out = tiles_product(count, col_at, row_to, pieces, source, UT, "users", "items", 1)
        kept, got = reduce_scatter(kept, out, "items")
        user_raw, sent = scale_panel(item_inverse, kept, got, user_scale)
        pieces = gather(sent, "items")
        user_inverse = inverse_factor(gram_sum(pieces, "users"), user_total)
        kept, out = tiles_product(count, row_at, col_to, pieces, tiles, IT, "items", "users", 0)
        kept, got = reduce_scatter(kept, out, "users")
        if step == ITERS - 1:
            user_panel = finish_panel(user_inverse, user_raw)
            user_panel, got = lax.optimization_barrier((user_panel, got))
        item_raw, sent = scale_panel(user_inverse, kept, got, item_scale)
    item_inverse = inverse_factor(all_sum(sent[0][-GRAM:].reshape(K // 2, TILE)), item_total)
    return user_panel, finish_panel(item_inverse, item_raw)


def solution(mesh):
    in_specs = (
        P("users", "items", None),
        P("users", "items", None),
        P("users", "items"),
        P("users", "items", None, None, None),
        P(("users", "items")),
        P(("items", "users")),
        P(None, ("items", "users")),
    )
    out_specs = (P(None, ("users", "items")), P(None, ("items", "users")))
    return jax.shard_map(body, mesh=mesh, in_specs=in_specs, out_specs=out_specs, check_vma=False)
```
